512 devices in a mesh: gy: 32 (over x, y_hi, core), gz: 16 (over y_lo, z).
Axes of the slice: x: 4, y: 8 (y_hi: 4, y_lo: 2; y = y_hi * 2 + y_lo), z: 8, core: 2. Of those that a mesh axis runs over, the one named last changes fastest.
Arguments:
- ckpt_pops: float32 [27, 64, 128, 128], P(None, 'gy', 'gz'), may hold values from 0 to 1, as said below
- adjoint_pops: float32 [27, 64, 128, 128], P(None, 'gy', 'gz'), may hold values from -8 to 8
- design: float32 [64, 128, 128], P('gy', 'gz'), may hold values from 0 to 1
- node_types: int32 [64, 128, 128], P('gy', 'gz'), may hold values from 0 to 3
Outputs:
- adjoint_prev: float32 [27, 64, 128, 128], P(None, 'gy', 'gz')
- sensitivity: float32 [64, 128, 128], P('gy', 'gz')
The draws below stay inside these ranges and needn't reach their ends.
Inputs may be any that keep to these rules, and one draw needn't show every extreme that they name: `ckpt_pops`: every population is positive.
All inputs are finite; a program needn't handle non-finite values.
Results may differ from the reference program's by a relative error of at most 0.0003.
Values sent between devices are 32-bit elements; how exact they have to be, the bound alone decides.
A program may use at most 64 MiB of HBM per device.

```python
import jax
import jax.numpy as jnp
import numpy as np
from jax import lax

NX = 128
RECOMP = 2
NY = 64
NZ = 128


def lattice_tables():
    index = np.arange(27)
    velocity = np.stack([index // 9 - 1, index // 3 % 3 - 1, index % 3 - 1], axis=1).astype(np.float32)
    single = np.array([1.0 / 6.0, 2.0 / 3.0, 1.0 / 6.0], np.float32)
    weights = single[index // 9] * single[index // 3 % 3] * single[index % 3]
    return (velocity, weights)


def draw_ckpt_pops(key, part):
    velocity, weights = lattice_tables()
    key_speed, key_mass, key_noise = jax.random.split(jax.random.fold_in(key, 11), 3)
    speeds = jax.random.uniform(key_speed, (3, NY, NZ, NX), jnp.float32, -0.1, 0.1)
    density = jax.random.uniform(key_mass, (NY, NZ, NX), jnp.float32, 0.9, 1.1)
    jitter = jax.random.uniform(key_noise, (27, NY, NZ, NX), jnp.float32, -0.2, 0.2)
    along = jnp.tensordot(jnp.asarray(velocity), speeds, axes=([1], [0]))
    squared = jnp.sum(speeds * speeds, axis=0)
    factor = 1.0 + 3.0 * along + 4.5 * along * along - 1.5 * squared + jitter
    return (jnp.asarray(weights)[:, None, None, None] * density * factor).astype(jnp.float32)


def draw_node_types(key, part):
    rolled = jax.random.randint(jax.random.fold_in(key, 23), (NY, NZ, NX), 0, 16)
    return jnp.where(rolled < 4, 1, jnp.where(rolled == 4, 2, jnp.where(rolled == 5, 3, 0))).astype(jnp.int32)


def steps_of(rng, dims, cuts, least, top_value):
    level, own = 1.0, jax.random.fold_in(rng, 6)
    for dim, blocks in cuts:
        heights = jnp.exp(jax.random.uniform(jax.random.fold_in(own, dim), (blocks,), jnp.float32, least / len(cuts), top_value / len(cuts)))
        level = level * jnp.repeat(heights, dims[dim] // blocks).reshape([-1 if axis == dim else 1 for axis in range(len(dims))])
    return level


def noise(own_key, extent, spread, bound, cuts=(), held_as=jnp.bfloat16):
    values = spread * jax.random.normal(own_key, extent, jnp.float32)
    if cuts:
        values = values * steps_of(own_key, extent, cuts, -0.22, 0.18)
    return jnp.clip(values, -bound, bound).astype(held_as)


def setup_inputs(seed: int = 0) -> dict:
    splits = jax.random.split(jax.random.key(seed), 5)
    ckpt_pops = draw_ckpt_pops(jax.random.fold_in(splits[4], 71), 0)
    adjoint_pops = noise(splits[1], (27, NY, NZ, NX), 2.0, 8.0, ((1, 32), (2, 16)), jnp.float32)
    design = jnp.clip(1.0 * jax.random.uniform(splits[2], (NY, NZ, NX), jnp.float32) ** steps_of(splits[2], (NY, NZ, NX), ((0, 32), (1, 16)), -0.2, 0.2), 0.0, 1.0)
    node_types = draw_node_types(jax.random.fold_in(splits[4], 71), 0)
    return dict(ckpt_pops=ckpt_pops, adjoint_pops=adjoint_pops, design=design, node_types=node_types)


relax_rate = 1.0 / 0.6
brinkman = 4.0
inflow = 0.05

def moment_line(values, shift):
    lower_v, middle, upper_v = (values[0], values[1], values[2])
    zeroth = lower_v + middle + upper_v
    linear = upper_v - lower_v - shift * zeroth
    square = upper_v + lower_v - 2.0 * shift * (upper_v - lower_v) + shift * shift * zeroth
    return jnp.stack([zeroth, linear, square])

def rebuild_line(moments, shift):
    zeroth, linear, square = (moments[0], moments[1], moments[2])
    lower_v = 0.5 * ((shift * shift - shift) * zeroth + (2.0 * shift - 1.0) * linear + square)
    middle = (1.0 - shift * shift) * zeroth - 2.0 * shift * linear - square
    upper_v = 0.5 * ((shift * shift + shift) * zeroth + (2.0 * shift + 1.0) * linear + square)
    return jnp.stack([lower_v, middle, upper_v])

def along_axis(values, axis_pos, func, shift):
    moved = jnp.moveaxis(values, axis_pos, 0)
    return jnp.moveaxis(func(moved, shift), 0, axis_pos)

def central(populations, speed_x, speed_y, speed_z):
    result = along_axis(populations, 0, moment_line, speed_x)
    result = along_axis(result, 1, moment_line, speed_y)
    return along_axis(result, 2, moment_line, speed_z)

def rebuild(moments, speed_x, speed_y, speed_z):
    result = along_axis(moments, 2, rebuild_line, speed_z)
    result = along_axis(result, 1, rebuild_line, speed_y)
    return along_axis(result, 0, rebuild_line, speed_x)

def gaussian_table(density, sxx, syy, szz, sxy, sxz, syz):
    nought = jnp.zeros_like(density)
    inverse = 1.0 / density
    entries = {(0, 0, 0): density, (2, 0, 0): sxx, (0, 2, 0): syy, (0, 0, 2): szz, (1, 1, 0): sxy, (1, 0, 1): sxz, (0, 1, 1): syz, (2, 2, 0): (sxx * syy + 2.0 * sxy * sxy) * inverse, (2, 0, 2): (sxx * szz + 2.0 * sxz * sxz) * inverse, (0, 2, 2): (syy * szz + 2.0 * syz * syz) * inverse, (2, 1, 1): (sxx * syz + 2.0 * sxy * sxz) * inverse, (1, 2, 1): (syy * sxz + 2.0 * sxy * syz) * inverse, (1, 1, 2): (szz * sxy + 2.0 * sxz * syz) * inverse, (2, 2, 2): (sxx * syy * szz + 2.0 * sxx * syz * syz + 2.0 * syy * sxz * sxz + 2.0 * szz * sxy * sxy + 8.0 * sxy * sxz * syz) * inverse * inverse}
    planes = []
    for first in range(3):
        row_list = []
        for second in range(3):
            row_list.append(jnp.stack([entries.get((first, second, third), nought) for third in range(3)]))
        planes.append(jnp.stack(row_list))
    return jnp.stack(planes)

def collide(populations, design, node):
    density = lax.optimization_barrier(jnp.sum(populations, axis=(0, 1, 2)))
    speed_x = (lax.optimization_barrier(jnp.sum(populations[2], axis=(0, 1))) - lax.optimization_barrier(jnp.sum(populations[0], axis=(0, 1)))) / density
    speed_y = (lax.optimization_barrier(jnp.sum(populations[:, 2], axis=(0, 1))) - lax.optimization_barrier(jnp.sum(populations[:, 0], axis=(0, 1)))) / density
    speed_z = (lax.optimization_barrier(jnp.sum(populations[:, :, 2], axis=(0, 1))) - lax.optimization_barrier(jnp.sum(populations[:, :, 0], axis=(0, 1)))) / density
    moments = central(populations, speed_x, speed_y, speed_z)
    third_rho = density / 3.0
    sxx = moments[2, 0, 0] + relax_rate * (third_rho - moments[2, 0, 0])
    syy = moments[0, 2, 0] + relax_rate * (third_rho - moments[0, 2, 0])
    szz = moments[0, 0, 2] + relax_rate * (third_rho - moments[0, 0, 2])
    sxy = (1.0 - relax_rate) * moments[1, 1, 0]
    sxz = (1.0 - relax_rate) * moments[1, 0, 1]
    syz = (1.0 - relax_rate) * moments[0, 1, 1]
    keeping = 1.0 / (1.0 + brinkman * (1.0 - design))
    fluid = rebuild(gaussian_table(density, sxx, syy, szz, sxy, sxz, syz), speed_x * keeping, speed_y * keeping, speed_z * keeping)
    unity = jnp.ones_like(density)
    nought = jnp.zeros_like(density)
    third = unity / 3.0
    resting = gaussian_table(unity, third, third, third, nought, nought, nought)
    outlet = rebuild(resting, speed_x, speed_y, speed_z)
    inlet = rebuild(resting, inflow * unity, nought, nought)
    bounce = populations[::-1, ::-1, ::-1]
    return jnp.where(node == 1, bounce, jnp.where(node == 2, inlet, jnp.where(node == 3, outlet, fluid)))

def collide_flat(flat, design_row, node_row):
    populations = flat.reshape((3, 3, 3) + flat.shape[1:])
    return collide(populations, design_row, node_row).reshape(flat.shape)

def propagate(values, sign):
    result = []
    for index in range(27):
        vel_x = index // 9 - 1
        vel_y = index // 3 % 3 - 1
        vel_z = index % 3 - 1
        result.append(jnp.roll(values[index], (sign * vel_y, sign * vel_z, sign * vel_x), axis=(0, 1, 2)))
    return jnp.stack(result)

def collide_grid(values, design, node_types):

    def one_row(packed):
        return collide_flat(packed[0], packed[1], packed[2])
    result = lax.map(one_row, (jnp.moveaxis(values, 1, 0), design, node_types))
    return jnp.moveaxis(result, 0, 1)

def reference(ckpt_pops, adjoint_pops, design, node_types):
    primal = ckpt_pops
    for step in range(RECOMP):
        primal = propagate(collide_grid(primal, design, node_types), 1)
    pulled = propagate(adjoint_pops, -1)

    def one_row(packed):
        flat_row, design_row, node_row, pulled_row = packed
        _, backward = jax.vjp(lambda popul, shape_field: collide_flat(popul, shape_field, node_row), flat_row, design_row)
        return backward(pulled_row)
    adjoint_rows, sensitivity = lax.map(one_row, (jnp.moveaxis(primal, 1, 0), design, node_types, jnp.moveaxis(pulled, 1, 0)))
    return (jnp.moveaxis(adjoint_rows, 0, 1), sensitivity)
```

```python
import jax
import jax.numpy as jnp
from jax import lax
from jax.experimental import pallas as pl
from jax.experimental.pallas import tpu as pltpu
from jax.sharding import PartitionSpec as P

relax_rate = 1.0 / 0.6
brinkman = 4.0
inflow = 0.05

MESH = pl.DeviceIdType.MESH
SIDES = [(1, 0), (-1, 0), (0, 1), (0, -1), (1, 1), (1, -1), (-1, 1), (-1, -1)]
KEPT = [(1, 0), (1, 1), (2, 0), (0, 1)]


def full(like, value):
    return jnp.full(like.shape, value, like.dtype)


def rebuild_line(zeroth, linear, square, shift):
    if zeroth is None:
        twice = shift * (linear + linear)
        if square is not None:
            twice = twice + square
        return 0.5 * (twice - linear), -twice, 0.5 * (twice + linear)
    odd = shift * zeroth
    if linear is None:
        even = shift * odd
    else:
        odd = odd + linear
        even = shift * (odd + linear)
    if square is not None:
        even = even + square
    return 0.5 * (even - odd), zeroth - even, 0.5 * (even + odd)


def collide(f, design, node):
    z0, z1, z2 = [], [], []
    for ab in range(9):
        lower, middle, upper = f[3 * ab : 3 * ab + 3]
        ends = upper + lower
        z0.append(ends + middle)
        z1.append(upper - lower)
        z2.append(ends)
    y00, y10, y20, y01, y11, y02 = [], [], [], [], [], []
    for a in range(3):
        ends = z0[3 * a + 2] + z0[3 * a]
        y00.append(ends + z0[3 * a + 1])
        y10.append(z0[3 * a + 2] - z0[3 * a])
        y20.append(ends)
        y01.append(z1[3 * a] + z1[3 * a + 1] + z1[3 * a + 2])
        y11.append(z1[3 * a + 2] - z1[3 * a])
        y02.append(z2[3 * a] + z2[3 * a + 1] + z2[3 * a + 2])
    m200 = y00[2] + y00[0]
    rho = m200 + y00[1]
    jx = y00[2] - y00[0]
    jy = y10[0] + y10[1] + y10[2]
    m110 = y10[2] - y10[0]
    m020 = y20[0] + y20[1] + y20[2]
    jz = y01[0] + y01[1] + y01[2]
    m101 = y01[2] - y01[0]
    m011 = y11[0] + y11[1] + y11[2]
    m002 = y02[0] + y02[1] + y02[2]

    inverse = 1.0 / rho
    ux, uy, uz = jx * inverse, jy * inverse, jz * inverse
    keep_rate = 1.0 - relax_rate
    base = (relax_rate / 3.0) * rho
    sxx = keep_rate * (m200 - jx * ux) + base
    syy = keep_rate * (m020 - jy * uy) + base
    szz = keep_rate * (m002 - jz * uz) + base
    sxy = keep_rate * (m110 - jx * uy)
    sxz = keep_rate * (m101 - jx * uz)
    syz = keep_rate * (m011 - jy * uz)

    fluid = node == 0
    one, nought, third = full(rho, 1.0), full(rho, 0.0), full(rho, 1.0 / 3.0)
    rho = lax.select(fluid, rho, one)
    inverse = lax.select(fluid, inverse, one)
    sxx = lax.select(fluid, sxx, third)
    syy = lax.select(fluid, syy, third)
    szz = lax.select(fluid, szz, third)
    sxy = lax.select(fluid, sxy, nought)
    sxz = lax.select(fluid, sxz, nought)
    syz = lax.select(fluid, syz, nought)
    keeping = 1.0 / (1.0 + brinkman * (1.0 - design))
    factor = lax.select(fluid, keeping, lax.select(node == 3, one, nought))
    vx = ux * factor + lax.select(node == 2, full(rho, inflow), nought)
    vy = uy * factor
    vz = uz * factor

    dxy, dxz, dyz = sxy + sxy, sxz + sxz, syz + syz
    fxy, fxz, fyz = dxy * sxy, dxz * sxz, dyz * syz
    g220 = (sxx * syy + fxy) * inverse
    g202 = (sxx * szz + fxz) * inverse
    g022 = (syy * szz + fyz) * inverse
    g211 = (sxx * syz + dxy * sxz) * inverse
    g121 = (syy * sxz + dxy * syz) * inverse
    g112 = (szz * sxy + dxz * syz) * inverse
    g222 = (
        (sxx * (syy * szz + fyz) + syy * fxz + szz * fxy + 2.0 * (dxy * dxz) * syz)
        * inverse
        * inverse
    )
    lines = {
        (0, 0): (rho, None, szz),
        (2, 0): (sxx, None, g202),
        (0, 2): (syy, None, g022),
        (2, 2): (g220, None, g222),
        (1, 1): (sxy, None, g112),
        (1, 0): (None, sxz, None),
        (0, 1): (None, syz, None),
        (2, 1): (None, g211, None),
        (1, 2): (None, g121, None),
    }
    along_z = {key: rebuild_line(*value, vz) for key, value in lines.items()}
    result = [None] * 27
    along_y = {
        (p, c): rebuild_line(along_z[p, 0][c], along_z[p, 1][c], along_z[p, 2][c], vy)
        for p in range(3)
        for c in range(3)
    }
    for b in range(3):
        for c in range(3):
            line = rebuild_line(along_y[0, c][b], along_y[1, c][b], along_y[2, c][b], vx)
            for a in range(3):
                result[9 * a + 3 * b + c] = line[a]
    solid = node == 1
    return [lax.select(solid, f[26 - i], result[i]) for i in range(27)]


def edge(step, last):
    return last if step > 0 else 0


def pack(tile, rows_z, rows_d):
    for way, step in enumerate((1, -1)):
        z, c = edge(step, 7), 1 + step
        for k, (b, y) in enumerate(KEPT):
            for a in range(3):
                rows_z[way, 3 * k + a : 3 * k + a + 1, :] = tile(a, b, c, y)[z : z + 1, :]
        for turn, step_y in enumerate((1, -1)):
            corner = 2 * turn + way
            for a in range(3):
                rows_d[corner, a : a + 1, :] = tile(a, 1 + step_y, c, edge(step_y, 1))[z : z + 1, :]


def arrive(tile, got_y, got_z, got_d, a, b, c, y, row):
    source = y - (b - 1)
    inside = 0 <= source < 2
    turn = 0 if b == 2 else 1
    value = tile(a, b, c, source) if inside else got_y[turn, a, c]
    if c != 1:
        way = 0 if c == 2 else 1
        if inside:
            k = 3 * KEPT.index((b, source)) + a
            line = got_z[way, k : k + 1, :]
        else:
            line = got_d[2 * turn + way, a : a + 1, :]
        value = pltpu.roll(value, 1 if c == 2 else 7, 0)
        value = jnp.where(row == (0 if c == 2 else 7), line, value)
    if a != 1:
        value = pltpu.roll(value, 1 if a == 2 else 127, 1)
    return value


def kernel(
    counts,
    ckpt,
    adjoint,
    design,
    node,
    previous,
    sensitivity,
    post,
    primal,
    pulled,
    got_y,
    put_z,
    got_z,
    put_d,
    got_d,
    send_sem,
    recv_sem,
):
    gy, gz = lax.axis_index("gy"), lax.axis_index("gz")
    near = [
        (lax.rem(gy + dy + counts[0], counts[0]), lax.rem(gz + dz + counts[1], counts[1]))
        for dy, dz in SIDES
    ]
    barrier = pltpu.get_barrier_semaphore()
    for who in near:
        pl.semaphore_signal(barrier, inc=1, device_id=who, device_id_type=MESH)

    def sends(turn, flat_y):
        sources = [
            (flat_y[0], got_y.at[turn, 0]),
            (flat_y[1], got_y.at[turn, 1]),
        ]
        sources += [(put_z.at[turn, way], got_z.at[turn, way]) for way in range(2)]
        sources += [(put_d.at[turn, way], got_d.at[turn, way]) for way in range(4)]
        copies = [
            pltpu.make_async_remote_copy(
                src_ref=src,
                dst_ref=dst,
                send_sem=send_sem.at[turn, i],
                recv_sem=recv_sem.at[turn, i],
                device_id=near[i],
                device_id_type=MESH,
            )
            for i, (src, dst) in enumerate(sources)
        ]
        for copy in reversed(copies):
            copy.start()
        return copies

    row = lax.broadcasted_iota(jnp.int32, (8, 128), 0)

    def collide_rows(load, turn):
        def body(y, carry):
            f = [load(i, y) for i in range(27)]
            h = collide(f, design[y], node[y])
            for i in range(27):
                post[turn, i // 3 % 3, y, i // 9, i % 3] = h[i]
            return carry

        lax.fori_loop(0, 2, body, 0)

    def post_tile(turn):
        return lambda a, b, c, y: post[turn, b, y, a, c]

    def gather(tile, turn, into, flip):
        for y in range(2):
            for i in range(27):
                a, b, c = i // 9, i // 3 % 3, i % 3
                value = arrive(
                    tile, got_y.at[turn], got_z.at[turn], got_d.at[turn], a, b, c, y, row
                )
                into[26 - i if flip else i, y] = value

    def adjoint_tile(a, b, c, y):
        return adjoint[2 - a, 2 - b, 2 - c, y]

    collide_rows(lambda i, y: ckpt[i // 9, i // 3 % 3, i % 3, y], 0)
    pack(post_tile(0), put_z.at[0], put_d.at[0])
    pl.semaphore_wait(barrier, len(near))
    first = sends(0, [post.at[0, 2, 1], post.at[0, 0, 0]])
    pack(adjoint_tile, put_z.at[2], put_d.at[2])
    third = sends(2, [adjoint.at[:, 0, :, 1], adjoint.at[:, 2, :, 0]])

    for copy in first:
        copy.wait_recv()
    gather(post_tile(0), 0, primal, False)

    collide_rows(lambda i, y: primal[i, y], 1)
    pack(post_tile(1), put_z.at[1], put_d.at[1])
    second = sends(1, [post.at[1, 2, 1], post.at[1, 0, 0]])

    for copy in third:
        copy.wait_recv()
    gather_adjoint(adjoint_tile, got_y.at[2], got_z.at[2], got_d.at[2], pulled, row)

    for copy in second:
        copy.wait_recv()
    gather(post_tile(1), 1, primal, False)

    def backward(y, carry):
        f = [primal[i, y] for i in range(27)]
        kind = node[y]
        _, pull = jax.vjp(lambda pops, field: collide(pops, field, kind), f, design[y])
        grads, slope = pull([pulled[i, y] for i in range(27)])
        for i in range(27):
            previous[i // 9, i // 3 % 3, i % 3, y] = grads[i]
        sensitivity[y] = slope
        return carry

    lax.fori_loop(0, 2, backward, 0)
    for copy in first + third + second:
        copy.wait_send()


class Reversed:
    def __init__(self, ref):
        self.ref = ref

    def __getitem__(self, key):
        turn, a, c = key
        return self.ref[turn, 2 - a, 2 - c]


def gather_adjoint(tile, got_y, got_z, got_d, into, row):
    for y in range(2):
        for i in range(27):
            a, b, c = i // 9, i // 3 % 3, i % 3
            value = arrive(tile, Reversed(got_y), got_z, got_d, a, b, c, y, row)
            into[26 - i, y] = value


def solution(mesh):
    counts = (mesh.shape["gy"], mesh.shape["gz"])

    def local(ckpt_pops, adjoint_pops, design, node_types):
        f32 = jnp.float32
        cells = ckpt_pops.shape[1:]
        whole = pl.BlockSpec(memory_space=pltpu.VMEM)
        previous, sensitivity = pl.pallas_call(
            lambda *refs: kernel(counts, *refs),
            out_shape=(
                jax.ShapeDtypeStruct((3, 3, 3) + cells, f32),
                jax.ShapeDtypeStruct(cells, f32),
            ),
            in_specs=[whole] * 4,
            out_specs=(whole, whole),
            scratch_shapes=[
                pltpu.VMEM((2, 3, 2, 3, 3, 8, 128), f32),
                pltpu.VMEM((27, 2, 8, 128), f32),
                pltpu.VMEM((27, 2, 8, 128), f32),
                pltpu.VMEM((3, 2, 3, 3, 8, 128), f32),
                pltpu.VMEM((3, 2, 16, 128), f32),
                pltpu.VMEM((3, 2, 16, 128), f32),
                pltpu.VMEM((3, 4, 8, 128), f32),
                pltpu.VMEM((3, 4, 8, 128), f32),
                pltpu.SemaphoreType.DMA((3, 8)),
                pltpu.SemaphoreType.DMA((3, 8)),
            ],
            compiler_params=pltpu.CompilerParams(collective_id=0, has_side_effects=True),
            name="adjoint_step",
        )(
            ckpt_pops.reshape((3, 3, 3) + cells),
            adjoint_pops.reshape((3, 3, 3) + cells),
            design,
            node_types,
        )
        return previous.reshape(ckpt_pops.shape), sensitivity

    return jax.shard_map(
        local,
        mesh=mesh,
        in_specs=(
            P(None, "gy", "gz", None),
            P(None, "gy", "gz", None),
            P("gy", "gz", None),
            P("gy", "gz", None),
        ),
        out_specs=(P(None, "gy", "gz", None), P("gy", "gz", None)),
        check_vma=False,
    )
```

```python
import jax
import jax.numpy as jnp
from jax import lax
from jax.experimental import pallas as pl
from jax.experimental.pallas import tpu as pltpu
from jax.sharding import PartitionSpec as P

relax_rate = 1.0 / 0.6
brinkman = 4.0
inflow = 0.05

MESH = pl.DeviceIdType.MESH
SIDES = [(1, 0), (-1, 0), (0, 1), (0, -1), (1, 1), (1, -1), (-1, 1), (-1, -1)]


def full(like, value):
    return jnp.full(like.shape, value, like.dtype)


def rebuild_line(zeroth, linear, square, shift):
    if zeroth is None:
        twice = shift * (linear + linear)
        if square is not None:
            twice = twice + square
        return 0.5 * (twice - linear), -twice, 0.5 * (twice + linear)
    odd = shift * zeroth
    if linear is None:
        even = shift * odd
    else:
        odd = odd + linear
        even = shift * (odd + linear)
    if square is not None:
        even = even + square
    return 0.5 * (even - odd), zeroth - even, 0.5 * (even + odd)


def collide(f, design, node):
    z0, z1, z2 = [], [], []
    for ab in range(9):
        lower, middle, upper = f[3 * ab : 3 * ab + 3]
        ends = upper + lower
        z0.append(ends + middle)
        z1.append(upper - lower)
        z2.append(ends)
    y00, y10, y20, y01, y11, y02 = [], [], [], [], [], []
    for a in range(3):
        ends = z0[3 * a + 2] + z0[3 * a]
        y00.append(ends + z0[3 * a + 1])
        y10.append(z0[3 * a + 2] - z0[3 * a])
        y20.append(ends)
        y01.append(z1[3 * a] + z1[3 * a + 1] + z1[3 * a + 2])
        y11.append(z1[3 * a + 2] - z1[3 * a])
        y02.append(z2[3 * a] + z2[3 * a + 1] + z2[3 * a + 2])
    m200 = y00[2] + y00[0]
    rho = m200 + y00[1]
    jx = y00[2] - y00[0]
    jy = y10[0] + y10[1] + y10[2]
    m110 = y10[2] - y10[0]
    m020 = y20[0] + y20[1] + y20[2]
    jz = y01[0] + y01[1] + y01[2]
    m101 = y01[2] - y01[0]
    m011 = y11[0] + y11[1] + y11[2]
    m002 = y02[0] + y02[1] + y02[2]

    inverse = 1.0 / rho
    ux, uy, uz = jx * inverse, jy * inverse, jz * inverse
    keep_rate = 1.0 - relax_rate
    base = (relax_rate / 3.0) * rho
    sxx = keep_rate * (m200 - jx * ux) + base
    syy = keep_rate * (m020 - jy * uy) + base
    szz = keep_rate * (m002 - jz * uz) + base
    sxy = keep_rate * (m110 - jx * uy)
    sxz = keep_rate * (m101 - jx * uz)
    syz = keep_rate * (m011 - jy * uz)

    fluid = node == 0
    one, nought, third = full(rho, 1.0), full(rho, 0.0), full(rho, 1.0 / 3.0)
    rho = lax.select(fluid, rho, one)
    inverse = lax.select(fluid, inverse, one)
    sxx = lax.select(fluid, sxx, third)
    syy = lax.select(fluid, syy, third)
    szz = lax.select(fluid, szz, third)
    sxy = lax.select(fluid, sxy, nought)
    sxz = lax.select(fluid, sxz, nought)
    syz = lax.select(fluid, syz, nought)
    keeping = 1.0 / (1.0 + brinkman * (1.0 - design))
    factor = lax.select(fluid, keeping, lax.select(node == 3, one, nought))
    vx = ux * factor + lax.select(node == 2, full(rho, inflow), nought)
    vy = uy * factor
    vz = uz * factor

    dxy, dxz, dyz = sxy + sxy, sxz + sxz, syz + syz
    fxy, fxz, fyz = dxy * sxy, dxz * sxz, dyz * syz
    g220 = (sxx * syy + fxy) * inverse
    g202 = (sxx * szz + fxz) * inverse
    g022 = (syy * szz + fyz) * inverse
    g211 = (sxx * syz + dxy * sxz) * inverse
    g121 = (syy * sxz + dxy * syz) * inverse
    g112 = (szz * sxy + dxz * syz) * inverse
    g222 = (
        (sxx * (syy * szz + fyz) + syy * fxz + szz * fxy + 2.0 * (dxy * dxz) * syz)
        * inverse
        * inverse
    )
    lines = {
        (0, 0): (rho, None, szz),
        (2, 0): (sxx, None, g202),
        (0, 2): (syy, None, g022),
        (2, 2): (g220, None, g222),
        (1, 1): (sxy, None, g112),
        (1, 0): (None, sxz, None),
        (0, 1): (None, syz, None),
        (2, 1): (None, g211, None),
        (1, 2): (None, g121, None),
    }
    along_z = {key: rebuild_line(*value, vz) for key, value in lines.items()}
    result = [None] * 27
    along_y = {
        (p, c): rebuild_line(along_z[p, 0][c], along_z[p, 1][c], along_z[p, 2][c], vy)
        for p in range(3)
        for c in range(3)
    }
    for b in range(3):
        for c in range(3):
            line = rebuild_line(along_y[0, c][b], along_y[1, c][b], along_y[2, c][b], vx)
            for a in range(3):
                result[9 * a + 3 * b + c] = line[a]
    solid = node == 1
    return [lax.select(solid, f[26 - i], result[i]) for i in range(27)]


def edge(step, last):
    return last if step > 0 else 0


GROUPS = {1: [(1, 1), (2, 0), (2, 1)], -1: [(0, 0), (0, 1), (1, 0)]}
CELL_ROW, BACK_ROW = 54, 58
KEPT = [(1, 0), (1, 1), (2, 0), (0, 1)]
TURNS = (1, -1)


def moving(step, kind):
    near, far = (7, 6) if step > 0 else (0, 1)
    return [(far, 1 + step), (near, 1), (near, 1 + step)][kind]


def pack(tile, back, design, node, rows_z, rows_d):
    for way, step in enumerate(TURNS):
        near = edge(step, 7)
        for kind in range(3):
            z, c = moving(step, kind)
            for y in range(2):
                for b in range(3):
                    for a in range(3):
                        k = 18 * kind + 9 * y + 3 * b + a
                        rows_z[way, k : k + 1, :] = tile(a, b, c, y)[z : z + 1, :]
        for y in range(2):
            k = CELL_ROW + 2 * y
            rows_z[way, k : k + 1, :] = design[y, near : near + 1, :]
            rows_z[way, k + 1 : k + 2, :] = node[y, near : near + 1, :].astype(jnp.float32)
        for k, (b, y) in enumerate(KEPT):
            for a in range(3):
                at = BACK_ROW + 3 * k + a
                rows_z[way, at : at + 1, :] = back(a, b, 1 + step, y)[near : near + 1, :]
        for turn, step_y in enumerate(TURNS):
            corner = 2 * turn + way
            for kind in range(3):
                z, c = moving(step, kind)
                for j, (b, y) in enumerate(GROUPS[step_y]):
                    for a in range(3):
                        k = 9 * kind + 3 * j + a
                        rows_d[corner, k : k + 1, :] = tile(a, b, c, y)[z : z + 1, :]
            y = edge(step_y, 1)
            rows_d[corner, 27:28, :] = design[y, near : near + 1, :]
            rows_d[corner, 28:29, :] = node[y, near : near + 1, :].astype(jnp.float32)
            for a in range(3):
                rows_d[corner, 29 + a : 30 + a, :] = back(a, 1 + step_y, 1 + step, y)[
                    near : near + 1, :
                ]


def shifted(value, a, c, line, row):
    if c != 1:
        value = pltpu.roll(value, 1 if c == 2 else 7, 0)
        value = jnp.where(row == (0 if c == 2 else 7), line, value)
    if a != 1:
        value = pltpu.roll(value, 1 if a == 2 else 127, 1)
    return value


def kernel(
    counts,
    ckpt,
    adjoint,
    design,
    node,
    previous,
    sensitivity,
    post,
    primal,
    wide_design,
    wide_node,
    ring_node,
    second,
    pulled,
    got_y,
    got_back,
    put_z,
    got_z,
    put_d,
    got_d,
    send_sem,
    recv_sem,
):
    gy, gz = lax.axis_index("gy"), lax.axis_index("gz")
    near = [
        (lax.rem(gy + dy + counts[0], counts[0]), lax.rem(gz + dz + counts[1], counts[1]))
        for dy, dz in SIDES
    ]
    barrier = pltpu.get_barrier_semaphore()
    for who in near:
        pl.semaphore_signal(barrier, inc=1, device_id=who, device_id_type=MESH)

    row = lax.broadcasted_iota(jnp.int32, (8, 128), 0)

    def collide_first(y, carry):
        f = [ckpt[i // 9, i // 3 % 3, i % 3, y] for i in range(27)]
        h = collide(f, design[y], node[y])
        for i in range(27):
            post[2 * (i // 3 % 3) + y, i // 9, i % 3] = h[i]
        return carry

    lax.fori_loop(0, 2, collide_first, 0)

    def own(a, b, c, y):
        return post[2 * b + y, a, c]

    def back(a, b, c, y):
        return adjoint[2 - a, 2 - b, 2 - c, y]

    pack(own, back, design, node, put_z, put_d)

    plan = [(put_d.at[i], got_d.at[i], 4 + i) for i in range(4)]
    plan += [(put_z.at[i], got_z.at[i], 2 + i) for i in range(2)]
    for turn, y in enumerate((1, 0)):
        plan += [
            (design.at[y], wide_design.at[3 * turn], turn),
            (node.at[y], ring_node.at[turn], turn),
        ]
    plan += [(post.at[pl.ds(3 - 3 * turn, 3)], got_y.at[turn], turn) for turn in range(2)]
    plan += [(adjoint.at[:, 2 * turn, :, 1 - turn], got_back.at[turn], turn) for turn in range(2)]
    copies = [
        pltpu.make_async_remote_copy(
            src_ref=src,
            dst_ref=dst,
            send_sem=send_sem.at[i],
            recv_sem=recv_sem.at[i],
            device_id=near[who],
            device_id_type=MESH,
        )
        for i, (src, dst, who) in enumerate(plan)
    ]
    pl.semaphore_wait(barrier, len(near))
    for copy in copies:
        copy.start()
    for copy in copies[:12]:
        copy.wait_recv()

    def outer(a, b, c, y):
        if 0 <= y < 2:
            return own(a, b, c, y)
        turn = 0 if y < 0 else 1
        return got_y[turn, GROUPS[TURNS[turn]].index((b, y + 2 if y < 0 else y - 2)), a, c]

    def edge_row(kind, a, b, y, way):
        if 0 <= y < 2:
            k = 18 * kind + 9 * y + 3 * b + a
            return got_z[way, k : k + 1, :]
        turn = 0 if y < 0 else 1
        j = GROUPS[TURNS[turn]].index((b, y + 2 if y < 0 else y - 2))
        k = 9 * kind + 3 * j + a
        return got_d[2 * turn + way, k : k + 1, :]

    def stack_rows(lines):
        value = jnp.broadcast_to(lines[0], (8, 128))
        for r in range(1, 8):
            value = jnp.where(row == r, lines[r], value)
        return value

    for i in range(27):
        a, b, c = i // 9, i // 3 % 3, i % 3
        for t in range(4):
            y = t - b
            line = None if c == 1 else edge_row(2, a, b, y, 0 if c == 2 else 1)
            primal[i, t] = shifted(outer(a, b, c, y), a, c, line, row)
        lines = []
        for way in range(2):
            for t in range(4):
                y = t - b
                if c == 1:
                    lines.append(edge_row(1, a, b, y, way))
                elif (c == 2) == (way == 0):
                    lines.append(edge_row(0, a, b, y, way))
                else:
                    z = 0 if way == 0 else 7
                    lines.append(outer(a, b, c, y)[z : z + 1, :])
        primal[i, 4] = shifted(stack_rows(lines), a, 1, None, row)
    for y in range(2):
        wide_design[1 + y] = design[y]
        wide_node[1 + y] = node[y]
    for turn in range(2):
        wide_node[3 * turn] = ring_node[turn]
    columns = []
    for part in range(2):
        lines = []
        for way in range(2):
            lines.append(got_d[way, 27 + part : 28 + part, :])
            for y in range(2):
                k = CELL_ROW + 2 * y + part
                lines.append(got_z[way, k : k + 1, :])
            lines.append(got_d[2 + way, 27 + part : 28 + part, :])
        columns.append(stack_rows(lines))
    wide_design[4] = columns[0]
    one, nought = jnp.ones_like(row), jnp.zeros_like(row)
    kind = jnp.where(columns[1] == 3.0, one + one + one, nought)
    kind = jnp.where(columns[1] == 2.0, one + one, kind)
    wide_node[4] = jnp.where(columns[1] == 1.0, one, kind)

    def collide_second(t, carry):
        f = [primal[i, t] for i in range(27)]
        h = collide(f, wide_design[t], wide_node[t])
        for i in range(27):
            second[i, t] = h[i]
        return carry

    lax.fori_loop(0, 5, collide_second, 0)

    for copy in copies[12:]:
        copy.wait_recv()
    for i in range(27):
        a, b, c = i // 9, i // 3 % 3, i % 3
        way = 0 if c == 2 else 1
        for y in range(2):
            t = y - b + 2
            r = t + 4 * way
            line = None if c == 1 else second[i, 4, r : r + 1, :]
            primal[i, y] = shifted(second[i, t], a, c, line, row)

            source = y - (b - 1)
            if 0 <= source < 2:
                value = back(a, b, c, source)
                k = BACK_ROW + 3 * KEPT.index((b, source)) + a if c != 1 else 0
                line = got_z[way, k : k + 1, :]
            else:
                turn = 0 if b == 2 else 1
                value = got_back[turn, 2 - a, 2 - c]
                line = got_d[2 * turn + way, 29 + a : 30 + a, :]
            pulled[26 - i, y] = shifted(value, a, c, line, row)

    def backward(y, carry):
        f = [primal[i, y] for i in range(27)]
        kind = node[y]
        _, pull = jax.vjp(lambda pops, field: collide(pops, field, kind), f, design[y])
        grads, slope = pull([pulled[i, y] for i in range(27)])
        for i in range(27):
            previous[i // 9, i // 3 % 3, i % 3, y] = grads[i]
        sensitivity[y] = slope
        return carry

    lax.fori_loop(0, 2, backward, 0)
    for copy in copies:
        copy.wait_send()


def solution(mesh):
    counts = (mesh.shape["gy"], mesh.shape["gz"])

    def local(ckpt_pops, adjoint_pops, design, node_types):
        f32 = jnp.float32
        cells = ckpt_pops.shape[1:]
        whole = pl.BlockSpec(memory_space=pltpu.VMEM)
        previous, sensitivity = pl.pallas_call(
            lambda *refs: kernel(counts, *refs),
            out_shape=(
                jax.ShapeDtypeStruct((3, 3, 3) + cells, f32),
                jax.ShapeDtypeStruct(cells, f32),
            ),
            in_specs=[whole] * 4,
            out_specs=(whole, whole),
            scratch_shapes=[
                pltpu.VMEM((6, 3, 3, 8, 128), f32),
                pltpu.VMEM((27, 5, 8, 128), f32),
                pltpu.VMEM((5, 8, 128), f32),
                pltpu.VMEM((5, 8, 128), jnp.int32),
                pltpu.VMEM((2, 8, 128), jnp.int32),
                pltpu.VMEM((27, 5, 8, 128), f32),
                pltpu.VMEM((27, 2, 8, 128), f32),
                pltpu.VMEM((2, 3, 3, 3, 8, 128), f32),
                pltpu.VMEM((2, 3, 3, 8, 128), f32),
                pltpu.VMEM((2, 72, 128), f32),
                pltpu.VMEM((2, 72, 128), f32),
                pltpu.VMEM((4, 32, 128), f32),
                pltpu.VMEM((4, 32, 128), f32),
                pltpu.SemaphoreType.DMA((14,)),
                pltpu.SemaphoreType.DMA((14,)),
            ],
            compiler_params=pltpu.CompilerParams(collective_id=0, has_side_effects=True),
            name="adjoint_step",
        )(
            ckpt_pops.reshape((3, 3, 3) + cells),
            adjoint_pops.reshape((3, 3, 3) + cells),
            design,
            node_types,
        )
        return previous.reshape(ckpt_pops.shape), sensitivity

    return jax.shard_map(
        local,
        mesh=mesh,
        in_specs=(
            P(None, "gy", "gz", None),
            P(None, "gy", "gz", None),
            P("gy", "gz", None),
            P("gy", "gz", None),
        ),
        out_specs=(P(None, "gy", "gz", None), P("gy", "gz", None)),
        check_vma=False,
    )
```

```python
import jax
import jax.numpy as jnp
from jax import lax
from jax.experimental import pallas as pl
from jax.experimental.pallas import tpu as pltpu
from jax.sharding import PartitionSpec as P

relax_rate = 1.0 / 0.6
brinkman = 4.0
inflow = 0.05

MESH = pl.DeviceIdType.MESH
SIDES = [(1, 0), (-1, 0), (0, 1), (0, -1), (1, 1), (1, -1), (-1, 1), (-1, -1)]


def full(like, value):
    return jnp.full(like.shape, value, like.dtype)


def rebuild_line(zeroth, linear, square, shift):
    if zeroth is None:
        twice = shift * (linear + linear)
        if square is not None:
            twice = twice + square
        return 0.5 * (twice - linear), -twice, 0.5 * (twice + linear)
    odd = shift * zeroth
    if linear is None:
        even = shift * odd
    else:
        odd = odd + linear
        even = shift * (odd + linear)
    if square is not None:
        even = even + square
    return 0.5 * (even - odd), zeroth - even, 0.5 * (even + odd)


def collide(f, design, node):
    z0, z1, z2 = [], [], []
    for ab in range(9):
        lower, middle, upper = f[3 * ab : 3 * ab + 3]
        ends = upper + lower
        z0.append(ends + middle)
        z1.append(upper - lower)
        z2.append(ends)
    y00, y10, y20, y01, y11, y02 = [], [], [], [], [], []
    for a in range(3):
        ends = z0[3 * a + 2] + z0[3 * a]
        y00.append(ends + z0[3 * a + 1])
        y10.append(z0[3 * a + 2] - z0[3 * a])
        y20.append(ends)
        y01.append(z1[3 * a] + z1[3 * a + 1] + z1[3 * a + 2])
        y11.append(z1[3 * a + 2] - z1[3 * a])
        y02.append(z2[3 * a] + z2[3 * a + 1] + z2[3 * a + 2])
    m200 = y00[2] + y00[0]
    rho = m200 + y00[1]
    jx = y00[2] - y00[0]
    jy = y10[0] + y10[1] + y10[2]
    m110 = y10[2] - y10[0]
    m020 = y20[0] + y20[1] + y20[2]
    jz = y01[0] + y01[1] + y01[2]
    m101 = y01[2] - y01[0]
    m011 = y11[0] + y11[1] + y11[2]
    m002 = y02[0] + y02[1] + y02[2]

    inverse = 1.0 / rho
    ux, uy, uz = jx * inverse, jy * inverse, jz * inverse
    keep_rate = 1.0 - relax_rate
    base = (relax_rate / 3.0) * rho
    sxx = keep_rate * (m200 - jx * ux) + base
    syy = keep_rate * (m020 - jy * uy) + base
    szz = keep_rate * (m002 - jz * uz) + base
    sxy = keep_rate * (m110 - jx * uy)
    sxz = keep_rate * (m101 - jx * uz)
    syz = keep_rate * (m011 - jy * uz)

    fluid = node == 0
    one, nought, third = full(rho, 1.0), full(rho, 0.0), full(rho, 1.0 / 3.0)
    rho = lax.select(fluid, rho, one)
    inverse = lax.select(fluid, inverse, one)
    sxx = lax.select(fluid, sxx, third)
    syy = lax.select(fluid, syy, third)
    szz = lax.select(fluid, szz, third)
    sxy = lax.select(fluid, sxy, nought)
    sxz = lax.select(fluid, sxz, nought)
    syz = lax.select(fluid, syz, nought)
    keeping = 1.0 / (1.0 + brinkman * (1.0 - design))
    factor = lax.select(fluid, keeping, lax.select(node == 3, one, nought))
    vx = ux * factor + lax.select(node == 2, full(rho, inflow), nought)
    vy = uy * factor
    vz = uz * factor

    dxy, dxz, dyz = sxy + sxy, sxz + sxz, syz + syz
    fxy, fxz, fyz = dxy * sxy, dxz * sxz, dyz * syz
    g220 = (sxx * syy + fxy) * inverse
    g202 = (sxx * szz + fxz) * inverse
    g022 = (syy * szz + fyz) * inverse
    g211 = (sxx * syz + dxy * sxz) * inverse
    g121 = (syy * sxz + dxy * syz) * inverse
    g112 = (szz * sxy + dxz * syz) * inverse
    g222 = (
        (sxx * (syy * szz + fyz) + syy * fxz + szz * fxy + 2.0 * (dxy * dxz) * syz)
        * inverse
        * inverse
    )
    lines = {
        (0, 0): (rho, None, szz),
        (2, 0): (sxx, None, g202),
        (0, 2): (syy, None, g022),
        (2, 2): (g220, None, g222),
        (1, 1): (sxy, None, g112),
        (1, 0): (None, sxz, None),
        (0, 1): (None, syz, None),
        (2, 1): (None, g211, None),
        (1, 2): (None, g121, None),
    }
    along_z = {key: rebuild_line(*value, vz) for key, value in lines.items()}
    result = [None] * 27
    along_y = {
        (p, c): rebuild_line(along_z[p, 0][c], along_z[p, 1][c], along_z[p, 2][c], vy)
        for p in range(3)
        for c in range(3)
    }
    for b in range(3):
        for c in range(3):
            line = rebuild_line(along_y[0, c][b], along_y[1, c][b], along_y[2, c][b], vx)
            for a in range(3):
                result[9 * a + 3 * b + c] = line[a]
    solid = node == 1
    return [lax.select(solid, f[26 - i], result[i]) for i in range(27)]


def edge(step, last):
    return last if step > 0 else 0


GROUPS = {1: [(1, 1), (2, 0), (2, 1)], -1: [(0, 0), (0, 1), (1, 0)]}
CELL_ROW, BACK_ROW = 54, 58
KEPT = [(1, 0), (1, 1), (2, 0), (0, 1)]
TURNS = (1, -1)


def moving(step, kind):
    near, far = (7, 6) if step > 0 else (0, 1)
    return [(far, 1 + step), (near, 1), (near, 1 + step)][kind]


def pack(tile, back, design, node, rows_z, rows_d):
    for way, step in enumerate(TURNS):
        near = edge(step, 7)
        for kind in range(3):
            z, c = moving(step, kind)
            for y in range(2):
                for b in range(3):
                    for a in range(3):
                        k = 18 * kind + 9 * y + 3 * b + a
                        rows_z[way, k : k + 1, :] = tile(a, b, c, y)[z : z + 1, :]
        for y in range(2):
            k = CELL_ROW + 2 * y
            rows_z[way, k : k + 1, :] = design[1 + y, near : near + 1, :]
            rows_z[way, k + 1 : k + 2, :] = node[1 + y, near : near + 1, :].astype(jnp.float32)
        for k, (b, y) in enumerate(KEPT):
            for a in range(3):
                at = BACK_ROW + 3 * k + a
                rows_z[way, at : at + 1, :] = back(a, b, 1 + step, y)[near : near + 1, :]
        for turn, step_y in enumerate(TURNS):
            corner = 2 * turn + way
            for kind in range(3):
                z, c = moving(step, kind)
                for j, (b, y) in enumerate(GROUPS[step_y]):
                    for a in range(3):
                        k = 9 * kind + 3 * j + a
                        rows_d[corner, k : k + 1, :] = tile(a, b, c, y)[z : z + 1, :]
            y = edge(step_y, 1)
            rows_d[corner, 27:28, :] = design[1 + y, near : near + 1, :]
            rows_d[corner, 28:29, :] = node[1 + y, near : near + 1, :].astype(jnp.float32)
            for a in range(3):
                rows_d[corner, 29 + a : 30 + a, :] = back(a, 1 + step_y, 1 + step, y)[
                    near : near + 1, :
                ]


def shifted(value, a, c, line, row):
    if c != 1:
        value = pltpu.roll(value, 1 if c == 2 else 7, 0)
        value = jnp.where(row == (0 if c == 2 else 7), line, value)
    if a != 1:
        value = pltpu.roll(value, 1 if a == 2 else 127, 1)
    return value


def gather_kernel(
    counts,
    ckpt_in,
    adjoint_in,
    design_in,
    node_in,
    final,
    pulled,
    design_out,
    node_out,
    ckpt,
    adjoint,
    post,
    primal,
    wide_design,
    wide_node,
    second,
    got_y,
    got_back,
    put_z,
    got_z,
    put_d,
    got_d,
    load_sem,
    send_sem,
    recv_sem,
):
    gy, gz = lax.axis_index("gy"), lax.axis_index("gz")
    near = [
        (lax.rem(gy + dy + counts[0], counts[0]), lax.rem(gz + dz + counts[1], counts[1]))
        for dy, dz in SIDES
    ]
    barrier = pltpu.get_barrier_semaphore()
    for who in near:
        pl.semaphore_signal(barrier, inc=1, device_id=who, device_id_type=MESH)

    loads = [
        pltpu.make_async_copy(src, dst, load_sem.at[i])
        for i, (src, dst) in enumerate(
            [
                (ckpt_in, ckpt),
                (design_in, wide_design.at[pl.ds(1, 2)]),
                (node_in, wide_node.at[pl.ds(1, 2)]),
                (adjoint_in, adjoint),
            ]
        )
    ]
    for load in loads:
        load.start()
    row = lax.broadcasted_iota(jnp.int32, (8, 128), 0)
    for load in loads[:3]:
        load.wait()

    def collide_first(y, carry):
        f = [ckpt[i // 9, i // 3 % 3, i % 3, y] for i in range(27)]
        h = collide(f, wide_design[1 + y], wide_node[1 + y])
        for i in range(27):
            post[2 * (i // 3 % 3) + y, i // 9, i % 3] = h[i]
        return carry

    lax.fori_loop(0, 2, collide_first, 0)

    def own(a, b, c, y):
        return post[2 * b + y, a, c]

    def back(a, b, c, y):
        return adjoint[2 - a, 2 - b, 2 - c, y]

    loads[3].wait()
    pack(own, back, wide_design, wide_node, put_z, put_d)

    plan = [(put_d.at[i], got_d.at[i], 4 + i) for i in range(4)]
    plan += [(put_z.at[i], got_z.at[i], 2 + i) for i in range(2)]
    for turn, y in enumerate((1, 0)):
        plan += [
            (wide_design.at[1 + y], wide_design.at[3 * turn], turn),
            (wide_node.at[1 + y], wide_node.at[3 * turn], turn),
        ]
    plan += [(post.at[pl.ds(3 - 3 * turn, 3)], got_y.at[turn], turn) for turn in range(2)]
    plan += [(adjoint.at[:, 2 * turn, :, 1 - turn], got_back.at[turn], turn) for turn in range(2)]
    copies = [
        pltpu.make_async_remote_copy(
            src_ref=src,
            dst_ref=dst,
            send_sem=send_sem.at[i],
            recv_sem=recv_sem.at[i],
            device_id=near[who],
            device_id_type=MESH,
        )
        for i, (src, dst, who) in enumerate(plan)
    ]
    pl.semaphore_wait(barrier, len(near))
    for copy in copies:
        copy.start()
    for copy in copies[:12]:
        copy.wait_recv()

    def outer(a, b, c, y):
        if 0 <= y < 2:
            return own(a, b, c, y)
        turn = 0 if y < 0 else 1
        return got_y[turn, GROUPS[TURNS[turn]].index((b, y + 2 if y < 0 else y - 2)), a, c]

    def edge_row(kind, a, b, y, way):
        if 0 <= y < 2:
            k = 18 * kind + 9 * y + 3 * b + a
            return got_z[way, k : k + 1, :]
        turn = 0 if y < 0 else 1
        j = GROUPS[TURNS[turn]].index((b, y + 2 if y < 0 else y - 2))
        k = 9 * kind + 3 * j + a
        return got_d[2 * turn + way, k : k + 1, :]

    def stack_rows(lines):
        value = jnp.broadcast_to(lines[0], (8, 128))
        for r in range(1, 8):
            value = jnp.where(row == r, lines[r], value)
        return value

    for i in range(27):
        a, b, c = i // 9, i // 3 % 3, i % 3
        for t in range(4):
            y = t - b
            line = None if c == 1 else edge_row(2, a, b, y, 0 if c == 2 else 1)
            primal[i, t] = shifted(outer(a, b, c, y), a, c, line, row)
        lines = []
        for way in range(2):
            for t in range(4):
                y = t - b
                if c == 1:
                    lines.append(edge_row(1, a, b, y, way))
                elif (c == 2) == (way == 0):
                    lines.append(edge_row(0, a, b, y, way))
                else:
                    z = 0 if way == 0 else 7
                    lines.append(outer(a, b, c, y)[z : z + 1, :])
        primal[i, 4] = shifted(stack_rows(lines), a, 1, None, row)
    columns = []
    for part in range(2):
        lines = []
        for way in range(2):
            lines.append(got_d[way, 27 + part : 28 + part, :])
            for y in range(2):
                k = CELL_ROW + 2 * y + part
                lines.append(got_z[way, k : k + 1, :])
            lines.append(got_d[2 + way, 27 + part : 28 + part, :])
        columns.append(stack_rows(lines))
    wide_design[4] = columns[0]
    one, nought = jnp.ones_like(row), jnp.zeros_like(row)
    kind = jnp.where(columns[1] == 3.0, one + one + one, nought)
    kind = jnp.where(columns[1] == 2.0, one + one, kind)
    wide_node[4] = jnp.where(columns[1] == 1.0, one, kind)

    def collide_second(t, carry):
        f = [primal[i, t] for i in range(27)]
        h = collide(f, wide_design[t], wide_node[t])
        for i in range(27):
            second[i, t] = h[i]
        return carry

    lax.fori_loop(0, 5, collide_second, 0)

    for copy in copies[12:]:
        copy.wait_recv()
    for i in range(27):
        a, b, c = i // 9, i // 3 % 3, i % 3
        way = 0 if c == 2 else 1
        for y in range(2):
            t = y - b + 2
            r = t + 4 * way
            line = None if c == 1 else second[i, 4, r : r + 1, :]
            final[i, y] = shifted(second[i, t], a, c, line, row)

            source = y - (b - 1)
            if 0 <= source < 2:
                value = back(a, b, c, source)
                k = BACK_ROW + 3 * KEPT.index((b, source)) + a if c != 1 else 0
                line = got_z[way, k : k + 1, :]
            else:
                turn = 0 if b == 2 else 1
                value = got_back[turn, 2 - a, 2 - c]
                line = got_d[2 * turn + way, 29 + a : 30 + a, :]
            pulled[26 - i, y] = shifted(value, a, c, line, row)

    for y in range(2):
        design_out[y] = wide_design[1 + y]
        node_out[y] = wide_node[1 + y]
    for copy in copies:
        copy.wait_send()


def backward_kernel(final, pulled, design, node, previous, sensitivity, grads, slopes, sem):
    copies = []
    for y in range(2):
        f = [final[i, y] for i in range(27)]
        kind = node[y]
        _, pull = jax.vjp(lambda pops, field, kind=kind: collide(pops, field, kind), f, design[y])
        values, slopes[y] = pull([pulled[i, y] for i in range(27)])
        for i in range(27):
            grads[y, i] = values[i]
        copies.append(pltpu.make_async_copy(grads.at[y], previous.at[:, y], sem.at[y]))
        copies[-1].start()
    copies.append(pltpu.make_async_copy(slopes, sensitivity, sem.at[2]))
    copies[-1].start()
    for copy in copies:
        copy.wait()


def solution(mesh):
    counts = (mesh.shape["gy"], mesh.shape["gz"])

    def local(ckpt_pops, adjoint_pops, design, node_types):
        f32 = jnp.float32
        cells = ckpt_pops.shape[1:]
        hbm = pl.BlockSpec(memory_space=pltpu.HBM)
        vmem = pl.BlockSpec(memory_space=pltpu.VMEM)
        slabs = (27,) + cells
        gathered = pl.pallas_call(
            lambda *refs: gather_kernel(counts, *refs),
            out_shape=(
                pltpu.VMEM(slabs, f32),
                pltpu.VMEM(slabs, f32),
                pltpu.VMEM(cells, f32),
                pltpu.VMEM(cells, jnp.int32),
            ),
            in_specs=[hbm] * 4,
            out_specs=[vmem] * 4,
            scratch_shapes=[
                pltpu.VMEM((3, 3, 3) + cells, f32),
                pltpu.VMEM((3, 3, 3) + cells, f32),
                pltpu.VMEM((6, 3, 3, 8, 128), f32),
                pltpu.VMEM((27, 5, 8, 128), f32),
                pltpu.VMEM((5, 8, 128), f32),
                pltpu.VMEM((5, 8, 128), jnp.int32),
                pltpu.VMEM((27, 5, 8, 128), f32),
                pltpu.VMEM((2, 3, 3, 3, 8, 128), f32),
                pltpu.VMEM((2, 3, 3, 8, 128), f32),
                pltpu.VMEM((2, 72, 128), f32),
                pltpu.VMEM((2, 72, 128), f32),
                pltpu.VMEM((4, 32, 128), f32),
                pltpu.VMEM((4, 32, 128), f32),
                pltpu.SemaphoreType.DMA((4,)),
                pltpu.SemaphoreType.DMA((14,)),
                pltpu.SemaphoreType.DMA((14,)),
            ],
            compiler_params=pltpu.CompilerParams(
                collective_id=0, has_side_effects=True, vmem_limit_bytes=16 * 2**20
            ),
            name="gather_cells",
        )(
            *[
                pltpu.with_memory_space_constraint(array, pltpu.HBM)
                for array in (
                    ckpt_pops.reshape((3, 3, 3) + cells),
                    adjoint_pops.reshape((3, 3, 3) + cells),
                    design,
                    node_types,
                )
            ]
        )
        return pl.pallas_call(
            backward_kernel,
            out_shape=(
                jax.ShapeDtypeStruct(slabs, f32),
                jax.ShapeDtypeStruct(cells, f32),
            ),
            in_specs=[vmem] * 4,
            out_specs=[hbm] * 2,
            scratch_shapes=[
                pltpu.VMEM((2, 27, 8, 128), f32),
                pltpu.VMEM((2, 8, 128), f32),
                pltpu.SemaphoreType.DMA((3,)),
            ],
            compiler_params=pltpu.CompilerParams(vmem_limit_bytes=16 * 2**20),
            name="backward_cells",
        )(*gathered)

    return jax.shard_map(
        local,
        mesh=mesh,
        in_specs=(
            P(None, "gy", "gz", None),
            P(None, "gy", "gz", None),
            P("gy", "gz", None),
            P("gy", "gz", None),
        ),
        out_specs=(P(None, "gy", "gz", None), P("gy", "gz", None)),
        check_vma=False,
    )
```

```python
import jax
import jax.numpy as jnp
from jax import lax
from jax.experimental import pallas as pl
from jax.experimental.pallas import tpu as pltpu
from jax.sharding import PartitionSpec as P

relax_rate = 1.0 / 0.6
brinkman = 4.0
inflow = 0.05

MESH = pl.DeviceIdType.MESH
SIDES = [(1, 0), (-1, 0), (0, 1), (0, -1)]


def full(like, value):
    return jnp.full(like.shape, value, like.dtype)


def rebuild_line(zeroth, linear, square, shift):
    if zeroth is None:
        twice = shift * (linear + linear)
        if square is not None:
            twice = twice + square
        return 0.5 * (twice - linear), -twice, 0.5 * (twice + linear)
    odd = shift * zeroth
    if linear is None:
        even = shift * odd
    else:
        odd = odd + linear
        even = shift * (odd + linear)
    if square is not None:
        even = even + square
    return 0.5 * (even - odd), zeroth - even, 0.5 * (even + odd)


def collide(f, design, node):
    z0, z1, z2 = [], [], []
    for ab in range(9):
        lower, middle, upper = f[3 * ab : 3 * ab + 3]
        ends = upper + lower
        z0.append(ends + middle)
        z1.append(upper - lower)
        z2.append(ends)
    y00, y10, y20, y01, y11, y02 = [], [], [], [], [], []
    for a in range(3):
        ends = z0[3 * a + 2] + z0[3 * a]
        y00.append(ends + z0[3 * a + 1])
        y10.append(z0[3 * a + 2] - z0[3 * a])
        y20.append(ends)
        y01.append(z1[3 * a] + z1[3 * a + 1] + z1[3 * a + 2])
        y11.append(z1[3 * a + 2] - z1[3 * a])
        y02.append(z2[3 * a] + z2[3 * a + 1] + z2[3 * a + 2])
    m200 = y00[2] + y00[0]
    rho = m200 + y00[1]
    jx = y00[2] - y00[0]
    jy = y10[0] + y10[1] + y10[2]
    m110 = y10[2] - y10[0]
    m020 = y20[0] + y20[1] + y20[2]
    jz = y01[0] + y01[1] + y01[2]
    m101 = y01[2] - y01[0]
    m011 = y11[0] + y11[1] + y11[2]
    m002 = y02[0] + y02[1] + y02[2]

    inverse = 1.0 / rho
    ux, uy, uz = jx * inverse, jy * inverse, jz * inverse
    keep_rate = 1.0 - relax_rate
    base = (relax_rate / 3.0) * rho
    sxx = keep_rate * (m200 - jx * ux) + base
    syy = keep_rate * (m020 - jy * uy) + base
    szz = keep_rate * (m002 - jz * uz) + base
    sxy = keep_rate * (m110 - jx * uy)
    sxz = keep_rate * (m101 - jx * uz)
    syz = keep_rate * (m011 - jy * uz)

    fluid = node == 0
    one, nought, third = full(rho, 1.0), full(rho, 0.0), full(rho, 1.0 / 3.0)
    rho = lax.select(fluid, rho, one)
    inverse = lax.select(fluid, inverse, one)
    sxx = lax.select(fluid, sxx, third)
    syy = lax.select(fluid, syy, third)
    szz = lax.select(fluid, szz, third)
    sxy = lax.select(fluid, sxy, nought)
    sxz = lax.select(fluid, sxz, nought)
    syz = lax.select(fluid, syz, nought)
    keeping = 1.0 / (1.0 + brinkman * (1.0 - design))
    factor = lax.select(fluid, keeping, lax.select(node == 3, one, nought))
    vx = ux * factor + lax.select(node == 2, full(rho, inflow), nought)
    vy = uy * factor
    vz = uz * factor

    dxy, dxz, dyz = sxy + sxy, sxz + sxz, syz + syz
    fxy, fxz, fyz = dxy * sxy, dxz * sxz, dyz * syz
    g220 = (sxx * syy + fxy) * inverse
    g202 = (sxx * szz + fxz) * inverse
    g022 = (syy * szz + fyz) * inverse
    g211 = (sxx * syz + dxy * sxz) * inverse
    g121 = (syy * sxz + dxy * syz) * inverse
    g112 = (szz * sxy + dxz * syz) * inverse
    g222 = (
        (sxx * (syy * szz + fyz) + syy * fxz + szz * fxy + 2.0 * (dxy * dxz) * syz)
        * inverse
        * inverse
    )
    lines = {
        (0, 0): (rho, None, szz),
        (2, 0): (sxx, None, g202),
        (0, 2): (syy, None, g022),
        (2, 2): (g220, None, g222),
        (1, 1): (sxy, None, g112),
        (1, 0): (None, sxz, None),
        (0, 1): (None, syz, None),
        (2, 1): (None, g211, None),
        (1, 2): (None, g121, None),
    }
    along_z = {key: rebuild_line(*value, vz) for key, value in lines.items()}
    result = [None] * 27
    along_y = {
        (p, c): rebuild_line(along_z[p, 0][c], along_z[p, 1][c], along_z[p, 2][c], vy)
        for p in range(3)
        for c in range(3)
    }
    for b in range(3):
        for c in range(3):
            line = rebuild_line(along_y[0, c][b], along_y[1, c][b], along_y[2, c][b], vx)
            for a in range(3):
                result[9 * a + 3 * b + c] = line[a]
    solid = node == 1
    return [lax.select(solid, f[26 - i], result[i]) for i in range(27)]


def edge(step, last):
    return last if step > 0 else 0


GROUPS = {1: [(1, 1), (2, 0), (2, 1)], -1: [(0, 0), (0, 1), (1, 0)]}
BACK_ROW = 64
KEPT = [(1, 0), (1, 1), (2, 0), (0, 1)]
TURNS = (1, -1)


def moving(step, kind):
    near, far = (7, 6) if step > 0 else (0, 1)
    return [(far, 1 + step), (near, 1), (near, 1 + step)][kind]


def pack(tile, back, design, node, rows):
    for way, step in enumerate(TURNS):
        near = edge(step, 7)
        for turn, step_y in enumerate(TURNS):
            base = 32 * turn
            for kind in range(3):
                z, c = moving(step, kind)
                for j, (b, y) in enumerate(GROUPS[step_y]):
                    for a in range(3):
                        k = base + 9 * kind + 3 * j + a
                        rows[way, k : k + 1, :] = tile(a, b, c, y)[z : z + 1, :]
            y, k = edge(step_y, 1), base + 27
            rows[way, k : k + 1, :] = design[1 + y, near : near + 1, :]
            rows[way, k + 1 : k + 2, :] = node[1 + y, near : near + 1, :].astype(jnp.float32)
            for a in range(3):
                k = base + 29 + a
                rows[way, k : k + 1, :] = back(a, 1 + step_y, 1 + step, y)[near : near + 1, :]
        for j, (b, y) in enumerate(KEPT):
            for a in range(3):
                k = BACK_ROW + 3 * j + a
                rows[way, k : k + 1, :] = back(a, b, 1 + step, y)[near : near + 1, :]


def shifted(value, a, c, line, row):
    if c != 1:
        value = pltpu.roll(value, 1 if c == 2 else 7, 0)
        value = jnp.where(row == (0 if c == 2 else 7), line, value)
    if a != 1:
        value = pltpu.roll(value, 1 if a == 2 else 127, 1)
    return value


def gather_kernel(
    counts,
    ckpt_in,
    adjoint_in,
    design_in,
    node_in,
    final,
    pulled,
    design_out,
    node_out,
    ckpt,
    adjoint,
    post,
    primal,
    wide_design,
    wide_node,
    second,
    got_y,
    got_back,
    put_z,
    got_z,
    got_d,
    load_sem,
    send_sem,
    recv_sem,
):
    gy, gz = lax.axis_index("gy"), lax.axis_index("gz")
    near = [
        (lax.rem(gy + dy + counts[0], counts[0]), lax.rem(gz + dz + counts[1], counts[1]))
        for dy, dz in SIDES
    ]
    barrier = pltpu.get_barrier_semaphore()
    for who in near:
        pl.semaphore_signal(barrier, inc=1, device_id=who, device_id_type=MESH)

    loads = [
        pltpu.make_async_copy(src, dst, load_sem.at[i])
        for i, (src, dst) in enumerate(
            [
                (ckpt_in, ckpt),
                (design_in, wide_design.at[pl.ds(1, 2)]),
                (node_in, wide_node.at[pl.ds(1, 2)]),
                (adjoint_in, adjoint),
            ]
        )
    ]
    for load in loads:
        load.start()
    row = lax.broadcasted_iota(jnp.int32, (8, 128), 0)
    for load in loads[:3]:
        load.wait()

    def collide_first(y, carry):
        f = [ckpt[i // 9, i // 3 % 3, i % 3, y] for i in range(27)]
        h = collide(f, wide_design[1 + y], wide_node[1 + y])
        for i in range(27):
            post[2 * (i // 3 % 3) + y, i // 9, i % 3] = h[i]
        return carry

    lax.fori_loop(0, 2, collide_first, 0)

    def own(a, b, c, y):
        return post[2 * b + y, a, c]

    def back(a, b, c, y):
        return adjoint[2 - a, 2 - b, 2 - c, y]

    loads[3].wait()
    pack(own, back, wide_design, wide_node, put_z)

    plan = [(put_z.at[i], got_z.at[i], 2 + i) for i in range(2)]
    for turn, y in enumerate((1, 0)):
        plan += [
            (wide_design.at[1 + y], wide_design.at[3 * turn], turn),
            (wide_node.at[1 + y], wide_node.at[3 * turn], turn),
        ]
    plan += [(post.at[pl.ds(3 - 3 * turn, 3)], got_y.at[turn], turn) for turn in range(2)]
    plan += [(adjoint.at[:, 2 * turn, :, 1 - turn], got_back.at[turn], turn) for turn in range(2)]
    plan += [
        (got_z.at[way, pl.ds(32 * turn, 32)], got_d.at[2 * turn + way], turn)
        for way in range(2)
        for turn in range(2)
    ]
    copies = [
        pltpu.make_async_remote_copy(
            src_ref=src,
            dst_ref=dst,
            send_sem=send_sem.at[i],
            recv_sem=recv_sem.at[i],
            device_id=near[who],
            device_id_type=MESH,
        )
        for i, (src, dst, who) in enumerate(plan)
    ]
    pl.semaphore_wait(barrier, len(near))
    for copy in copies[:10]:
        copy.start()
    for way in range(2):
        copies[way].wait_recv()
        for copy in copies[10 + 2 * way : 12 + 2 * way]:
            copy.start()
    for copy in copies[2:8] + copies[10:]:
        copy.wait_recv()

    def outer(a, b, c, y):
        if 0 <= y < 2:
            return own(a, b, c, y)
        turn = 0 if y < 0 else 1
        return got_y[turn, GROUPS[TURNS[turn]].index((b, y + 2 if y < 0 else y - 2)), a, c]

    def edge_row(kind, a, b, y, way):
        turn = 0 if y < 0 or y < 2 and (b, y) in GROUPS[1] else 1
        j = GROUPS[TURNS[turn]].index((b, y % 2))
        k = 9 * kind + 3 * j + a
        if 0 <= y < 2:
            return got_z[way, 32 * turn + k : 32 * turn + k + 1, :]
        return got_d[2 * turn + way, k : k + 1, :]

    def stack_rows(lines):
        value = jnp.broadcast_to(lines[0], (8, 128))
        for r in range(1, 8):
            value = jnp.where(row == r, lines[r], value)
        return value

    for i in range(27):
        a, b, c = i // 9, i // 3 % 3, i % 3
        for t in range(4):
            y = t - b
            line = None if c == 1 else edge_row(2, a, b, y, 0 if c == 2 else 1)
            primal[i, t] = shifted(outer(a, b, c, y), a, c, line, row)
        lines = []
        for way in range(2):
            for t in range(4):
                y = t - b
                if c == 1:
                    lines.append(edge_row(1, a, b, y, way))
                elif (c == 2) == (way == 0):
                    lines.append(edge_row(0, a, b, y, way))
                else:
                    z = 0 if way == 0 else 7
                    lines.append(outer(a, b, c, y)[z : z + 1, :])
        primal[i, 4] = shifted(stack_rows(lines), a, 1, None, row)
    columns = []
    for part in range(2):
        lines = []
        for way in range(2):
            lines.append(got_d[way, 27 + part : 28 + part, :])
            for y in range(2):
                k = 32 * (1 - y) + 27 + part
                lines.append(got_z[way, k : k + 1, :])
            lines.append(got_d[2 + way, 27 + part : 28 + part, :])
        columns.append(stack_rows(lines))
    wide_design[4] = columns[0]
    one, nought = jnp.ones_like(row), jnp.zeros_like(row)
    kind = jnp.where(columns[1] == 3.0, one + one + one, nought)
    kind = jnp.where(columns[1] == 2.0, one + one, kind)
    wide_node[4] = jnp.where(columns[1] == 1.0, one, kind)

    def collide_second(t, carry):
        f = [primal[i, t] for i in range(27)]
        h = collide(f, wide_design[t], wide_node[t])
        for i in range(27):
            second[i, t] = h[i]
        return carry

    lax.fori_loop(0, 5, collide_second, 0)

    for copy in copies[8:10]:
        copy.wait_recv()
    for i in range(27):
        a, b, c = i // 9, i // 3 % 3, i % 3
        way = 0 if c == 2 else 1
        for y in range(2):
            t = y - b + 2
            r = t + 4 * way
            line = None if c == 1 else second[i, 4, r : r + 1, :]
            final[i, y] = shifted(second[i, t], a, c, line, row)

            source = y - (b - 1)
            if 0 <= source < 2:
                value = back(a, b, c, source)
                k = BACK_ROW + 3 * KEPT.index((b, source)) + a if c != 1 else 0
                line = got_z[way, k : k + 1, :]
            else:
                turn = 0 if b == 2 else 1
                value = got_back[turn, 2 - a, 2 - c]
                line = got_d[2 * turn + way, 29 + a : 30 + a, :]
            pulled[26 - i, y] = shifted(value, a, c, line, row)

    for y in range(2):
        design_out[y] = wide_design[1 + y]
        node_out[y] = wide_node[1 + y]
    for copy in copies:
        copy.wait_send()


def backward_kernel(final, pulled, design, node, previous, sensitivity, grads, slopes, sem):
    copies = []
    for y in range(2):
        f = [final[i, y] for i in range(27)]
        kind = node[y]
        _, pull = jax.vjp(lambda pops, field, kind=kind: collide(pops, field, kind), f, design[y])
        values, slopes[y] = pull([pulled[i, y] for i in range(27)])
        for i in range(27):
            grads[y, i] = values[i]
        copies.append(pltpu.make_async_copy(grads.at[y], previous.at[:, y], sem.at[y]))
        copies[-1].start()
    copies.append(pltpu.make_async_copy(slopes, sensitivity, sem.at[2]))
    copies[-1].start()
    for copy in copies:
        copy.wait()


def solution(mesh):
    counts = (mesh.shape["gy"], mesh.shape["gz"])

    def local(ckpt_pops, adjoint_pops, design, node_types):
        f32 = jnp.float32
        cells = ckpt_pops.shape[1:]
        hbm = pl.BlockSpec(memory_space=pltpu.HBM)
        vmem = pl.BlockSpec(memory_space=pltpu.VMEM)
        slabs = (27,) + cells
        gathered = pl.pallas_call(
            lambda *refs: gather_kernel(counts, *refs),
            out_shape=(
                pltpu.VMEM(slabs, f32),
                pltpu.VMEM(slabs, f32),
                pltpu.VMEM(cells, f32),
                pltpu.VMEM(cells, jnp.int32),
            ),
            in_specs=[hbm] * 4,
            out_specs=[vmem] * 4,
            scratch_shapes=[
                pltpu.VMEM((3, 3, 3) + cells, f32),
                pltpu.VMEM((3, 3, 3) + cells, f32),
                pltpu.VMEM((6, 3, 3, 8, 128), f32),
                pltpu.VMEM((27, 5, 8, 128), f32),
                pltpu.VMEM((5, 8, 128), f32),
                pltpu.VMEM((5, 8, 128), jnp.int32),
                pltpu.VMEM((27, 5, 8, 128), f32),
                pltpu.VMEM((2, 3, 3, 3, 8, 128), f32),
                pltpu.VMEM((2, 3, 3, 8, 128), f32),
                pltpu.VMEM((2, 80, 128), f32),
                pltpu.VMEM((2, 80, 128), f32),
                pltpu.VMEM((4, 32, 128), f32),
                pltpu.SemaphoreType.DMA((4,)),
                pltpu.SemaphoreType.DMA((14,)),
                pltpu.SemaphoreType.DMA((14,)),
            ],
            compiler_params=pltpu.CompilerParams(
                collective_id=0, has_side_effects=True, vmem_limit_bytes=16 * 2**20
            ),
            name="gather_cells",
        )(
            *[
                pltpu.with_memory_space_constraint(array, pltpu.HBM)
                for array in (
                    ckpt_pops.reshape((3, 3, 3) + cells),
                    adjoint_pops.reshape((3, 3, 3) + cells),
                    design,
                    node_types,
                )
            ]
        )
        return pl.pallas_call(
            backward_kernel,
            out_shape=(
                jax.ShapeDtypeStruct(slabs, f32),
                jax.ShapeDtypeStruct(cells, f32),
            ),
            in_specs=[vmem] * 4,
            out_specs=[hbm] * 2,
            scratch_shapes=[
                pltpu.VMEM((2, 27, 8, 128), f32),
                pltpu.VMEM((2, 8, 128), f32),
                pltpu.SemaphoreType.DMA((3,)),
            ],
            compiler_params=pltpu.CompilerParams(vmem_limit_bytes=16 * 2**20),
            name="backward_cells",
        )(*gathered)

    return jax.shard_map(
        local,
        mesh=mesh,
        in_specs=(
            P(None, "gy", "gz", None),
            P(None, "gy", "gz", None),
            P("gy", "gz", None),
            P("gy", "gz", None),
        ),
        out_specs=(P(None, "gy", "gz", None), P("gy", "gz", None)),
        check_vma=False,
    )
```

```python
import jax
import jax.numpy as jnp
from jax import lax
from jax.experimental import pallas as pl
from jax.experimental.pallas import tpu as pltpu
from jax.sharding import PartitionSpec as P

relax_rate = 1.0 / 0.6
brinkman = 4.0
inflow = 0.05

MESH = pl.DeviceIdType.MESH
SIDES = [(1, 0), (-1, 0), (0, 1), (0, -1)]


def full(like, value):
    return jnp.full(like.shape, value, like.dtype)


def rebuild_line(zeroth, linear, square, shift):
    if zeroth is None:
        twice = shift * (linear + linear)
        if square is not None:
            twice = twice + square
        return 0.5 * (twice - linear), -twice, 0.5 * (twice + linear)
    odd = shift * zeroth
    if linear is None:
        even = shift * odd
    else:
        odd = odd + linear
        even = shift * (odd + linear)
    if square is not None:
        even = even + square
    return 0.5 * (even - odd), zeroth - even, 0.5 * (even + odd)


def collide(f, design, node):
    z0, z1, z2 = [], [], []
    for ab in range(9):
        lower, middle, upper = f[3 * ab : 3 * ab + 3]
        ends = upper + lower
        z0.append(ends + middle)
        z1.append(upper - lower)
        z2.append(ends)
    y00, y10, y20, y01, y11, y02 = [], [], [], [], [], []
    for a in range(3):
        ends = z0[3 * a + 2] + z0[3 * a]
        y00.append(ends + z0[3 * a + 1])
        y10.append(z0[3 * a + 2] - z0[3 * a])
        y20.append(ends)
        y01.append(z1[3 * a] + z1[3 * a + 1] + z1[3 * a + 2])
        y11.append(z1[3 * a + 2] - z1[3 * a])
        y02.append(z2[3 * a] + z2[3 * a + 1] + z2[3 * a + 2])
    m200 = y00[2] + y00[0]
    rho = m200 + y00[1]
    jx = y00[2] - y00[0]
    jy = y10[0] + y10[1] + y10[2]
    m110 = y10[2] - y10[0]
    m020 = y20[0] + y20[1] + y20[2]
    jz = y01[0] + y01[1] + y01[2]
    m101 = y01[2] - y01[0]
    m011 = y11[0] + y11[1] + y11[2]
    m002 = y02[0] + y02[1] + y02[2]

    inverse = 1.0 / rho
    ux, uy, uz = jx * inverse, jy * inverse, jz * inverse
    keep_rate = 1.0 - relax_rate
    base = (relax_rate / 3.0) * rho
    sxx = keep_rate * (m200 - jx * ux) + base
    syy = keep_rate * (m020 - jy * uy) + base
    szz = keep_rate * (m002 - jz * uz) + base
    sxy = keep_rate * (m110 - jx * uy)
    sxz = keep_rate * (m101 - jx * uz)
    syz = keep_rate * (m011 - jy * uz)

    fluid = node == 0
    one, nought, third = full(rho, 1.0), full(rho, 0.0), full(rho, 1.0 / 3.0)
    rho = lax.select(fluid, rho, one)
    inverse = lax.select(fluid, inverse, one)
    sxx = lax.select(fluid, sxx, third)
    syy = lax.select(fluid, syy, third)
    szz = lax.select(fluid, szz, third)
    sxy = lax.select(fluid, sxy, nought)
    sxz = lax.select(fluid, sxz, nought)
    syz = lax.select(fluid, syz, nought)
    keeping = 1.0 / (1.0 + brinkman * (1.0 - design))
    factor = lax.select(fluid, keeping, lax.select(node == 3, one, nought))
    vx = ux * factor + lax.select(node == 2, full(rho, inflow), nought)
    vy = uy * factor
    vz = uz * factor

    dxy, dxz, dyz = sxy + sxy, sxz + sxz, syz + syz
    fxy, fxz, fyz = dxy * sxy, dxz * sxz, dyz * syz
    g220 = (sxx * syy + fxy) * inverse
    g202 = (sxx * szz + fxz) * inverse
    g022 = (syy * szz + fyz) * inverse
    g211 = (sxx * syz + dxy * sxz) * inverse
    g121 = (syy * sxz + dxy * syz) * inverse
    g112 = (szz * sxy + dxz * syz) * inverse
    g222 = (
        (sxx * (syy * szz + fyz) + syy * fxz + szz * fxy + 2.0 * (dxy * dxz) * syz)
        * inverse
        * inverse
    )
    lines = {
        (0, 0): (rho, None, szz),
        (2, 0): (sxx, None, g202),
        (0, 2): (syy, None, g022),
        (2, 2): (g220, None, g222),
        (1, 1): (sxy, None, g112),
        (1, 0): (None, sxz, None),
        (0, 1): (None, syz, None),
        (2, 1): (None, g211, None),
        (1, 2): (None, g121, None),
    }
    along_z = {key: rebuild_line(*value, vz) for key, value in lines.items()}
    result = [None] * 27
    along_y = {
        (p, c): rebuild_line(along_z[p, 0][c], along_z[p, 1][c], along_z[p, 2][c], vy)
        for p in range(3)
        for c in range(3)
    }
    for b in range(3):
        for c in range(3):
            line = rebuild_line(along_y[0, c][b], along_y[1, c][b], along_y[2, c][b], vx)
            for a in range(3):
                result[9 * a + 3 * b + c] = line[a]
    solid = node == 1
    return [lax.select(solid, f[26 - i], result[i]) for i in range(27)]


def edge(step, last):
    return last if step > 0 else 0


GROUPS = {1: [(1, 1), (2, 0), (2, 1)], -1: [(0, 0), (0, 1), (1, 0)]}
BACK_ROW = 64
KEPT = [(1, 0), (1, 1), (2, 0), (0, 1)]
TURNS = (1, -1)


def moving(step, kind):
    near, far = (7, 6) if step > 0 else (0, 1)
    return [(far, 1 + step), (near, 1), (near, 1 + step)][kind]


def pack(tile, back, design, node, rows):
    for way, step in enumerate(TURNS):
        near = edge(step, 7)
        for turn, step_y in enumerate(TURNS):
            base = 32 * turn
            for kind in range(3):
                z, c = moving(step, kind)
                for j, (b, y) in enumerate(GROUPS[step_y]):
                    for a in range(3):
                        k = base + 9 * kind + 3 * j + a
                        rows[way, k : k + 1, :] = tile(a, b, c, y)[z : z + 1, :]
            y, k = edge(step_y, 1), base + 27
            rows[way, k : k + 1, :] = design[1 + y, near : near + 1, :]
            rows[way, k + 1 : k + 2, :] = node[1 + y, near : near + 1, :].astype(jnp.float32)
            for a in range(3):
                k = base + 29 + a
                rows[way, k : k + 1, :] = back(a, 1 + step_y, 1 + step, y)[near : near + 1, :]
        for j, (b, y) in enumerate(KEPT):
            for a in range(3):
                k = BACK_ROW + 3 * j + a
                rows[way, k : k + 1, :] = back(a, b, 1 + step, y)[near : near + 1, :]


def shifted(value, a, c, line, row):
    if c != 1:
        value = pltpu.roll(value, 1 if c == 2 else 7, 0)
        value = jnp.where(row == (0 if c == 2 else 7), line, value)
    if a != 1:
        value = pltpu.roll(value, 1 if a == 2 else 127, 1)
    return value


def gather_kernel(
    counts,
    ckpt_in,
    adjoint_in,
    design_in,
    node_in,
    final,
    pulled,
    design_out,
    node_out,
    ckpt,
    adjoint,
    post,
    primal,
    wide_design,
    wide_node,
    second,
    got_y,
    got_back,
    put_z,
    got_z,
    got_d,
    load_sem,
    send_sem,
    recv_sem,
):
    gy, gz = lax.axis_index("gy"), lax.axis_index("gz")
    near = [
        (lax.rem(gy + dy + counts[0], counts[0]), lax.rem(gz + dz + counts[1], counts[1]))
        for dy, dz in SIDES
    ]
    barrier = pltpu.get_barrier_semaphore()
    for who in near:
        pl.semaphore_signal(barrier, inc=1, device_id=who, device_id_type=MESH)

    loads = [
        pltpu.make_async_copy(src, dst, load_sem.at[i])
        for i, (src, dst) in enumerate(
            [
                (ckpt_in, ckpt),
                (design_in, wide_design.at[pl.ds(1, 2)]),
                (node_in, wide_node.at[pl.ds(1, 2)]),
                (adjoint_in, adjoint),
            ]
        )
    ]
    for load in loads:
        load.start()
    row = lax.broadcasted_iota(jnp.int32, (8, 128), 0)
    for load in loads[:3]:
        load.wait()

    def collide_first(y, carry):
        f = [ckpt[i // 9, i // 3 % 3, i % 3, y] for i in range(27)]
        h = collide(f, wide_design[1 + y], wide_node[1 + y])
        for i in range(27):
            post[2 * (i // 3 % 3) + y, i // 9, i % 3] = h[i]
        return carry

    lax.fori_loop(0, 2, collide_first, 0)

    def own(a, b, c, y):
        return post[2 * b + y, a, c]

    def back(a, b, c, y):
        return adjoint[2 - a, 2 - b, 2 - c, y]

    loads[3].wait()
    pack(own, back, wide_design, wide_node, put_z)

    parts = [(way, pl.ds(32 * turn, 32), turn) for way in range(2) for turn in range(2)]
    stay = pl.ds(BACK_ROW, 16)
    plan = [(put_z.at[way, part], got_z.at[way, part], 2 + way) for way, part, _ in parts]
    for turn, y in enumerate((1, 0)):
        plan += [
            (wide_design.at[1 + y], wide_design.at[3 * turn], turn),
            (wide_node.at[1 + y], wide_node.at[3 * turn], turn),
        ]
    plan += [(post.at[pl.ds(3 - 3 * turn, 3)], got_y.at[turn], turn) for turn in range(2)]
    plan += [(adjoint.at[:, 2 * turn, :, 1 - turn], got_back.at[turn], turn) for turn in range(2)]
    plan += [(put_z.at[way, stay], got_z.at[way, stay], 2 + way) for way in range(2)]
    plan += [(got_z.at[way, part], got_d.at[2 * turn + way], turn) for way, part, turn in parts]
    copies = [
        pltpu.make_async_remote_copy(
            src_ref=src,
            dst_ref=dst,
            send_sem=send_sem.at[i],
            recv_sem=recv_sem.at[i],
            device_id=near[who],
            device_id_type=MESH,
        )
        for i, (src, dst, who) in enumerate(plan)
    ]
    pl.semaphore_wait(barrier, len(near))
    for copy in copies[:14]:
        copy.start()
    for k in range(4):
        copies[k].wait_recv()
        copies[14 + k].start()
    for copy in copies[4:10] + copies[14:]:
        copy.wait_recv()

    def outer(a, b, c, y):
        if 0 <= y < 2:
            return own(a, b, c, y)
        turn = 0 if y < 0 else 1
        return got_y[turn, GROUPS[TURNS[turn]].index((b, y + 2 if y < 0 else y - 2)), a, c]

    def edge_row(kind, a, b, y, way):
        turn = 0 if y < 0 or y < 2 and (b, y) in GROUPS[1] else 1
        j = GROUPS[TURNS[turn]].index((b, y % 2))
        k = 9 * kind + 3 * j + a
        if 0 <= y < 2:
            return got_z[way, 32 * turn + k : 32 * turn + k + 1, :]
        return got_d[2 * turn + way, k : k + 1, :]

    def stack_rows(lines):
        value = jnp.broadcast_to(lines[0], (8, 128))
        for r in range(1, 8):
            value = jnp.where(row == r, lines[r], value)
        return value

    for i in range(27):
        a, b, c = i // 9, i // 3 % 3, i % 3
        for t in range(4):
            y = t - b
            line = None if c == 1 else edge_row(2, a, b, y, 0 if c == 2 else 1)
            primal[i, t] = shifted(outer(a, b, c, y), a, c, line, row)
        lines = []
        for way in range(2):
            for t in range(4):
                y = t - b
                if c == 1:
                    lines.append(edge_row(1, a, b, y, way))
                elif (c == 2) == (way == 0):
                    lines.append(edge_row(0, a, b, y, way))
                else:
                    z = 0 if way == 0 else 7
                    lines.append(outer(a, b, c, y)[z : z + 1, :])
        primal[i, 4] = shifted(stack_rows(lines), a, 1, None, row)
    columns = []
    for part in range(2):
        lines = []
        for way in range(2):
            lines.append(got_d[way, 27 + part : 28 + part, :])
            for y in range(2):
                k = 32 * (1 - y) + 27 + part
                lines.append(got_z[way, k : k + 1, :])
            lines.append(got_d[2 + way, 27 + part : 28 + part, :])
        columns.append(stack_rows(lines))
    wide_design[4] = columns[0]
    one, nought = jnp.ones_like(row), jnp.zeros_like(row)
    kind = jnp.where(columns[1] == 3.0, one + one + one, nought)
    kind = jnp.where(columns[1] == 2.0, one + one, kind)
    wide_node[4] = jnp.where(columns[1] == 1.0, one, kind)

    def collide_second(t, carry):
        f = [primal[i, t] for i in range(27)]
        h = collide(f, wide_design[t], wide_node[t])
        for i in range(27):
            second[i, t] = h[i]
        return carry

    lax.fori_loop(0, 5, collide_second, 0)

    for copy in copies[10:14]:
        copy.wait_recv()
    for i in range(27):
        a, b, c = i // 9, i // 3 % 3, i % 3
        way = 0 if c == 2 else 1
        for y in range(2):
            t = y - b + 2
            r = t + 4 * way
            line = None if c == 1 else second[i, 4, r : r + 1, :]
            final[i, y] = shifted(second[i, t], a, c, line, row)

            source = y - (b - 1)
            if 0 <= source < 2:
                value = back(a, b, c, source)
                k = BACK_ROW + 3 * KEPT.index((b, source)) + a if c != 1 else 0
                line = got_z[way, k : k + 1, :]
            else:
                turn = 0 if b == 2 else 1
                value = got_back[turn, 2 - a, 2 - c]
                line = got_d[2 * turn + way, 29 + a : 30 + a, :]
            pulled[26 - i, y] = shifted(value, a, c, line, row)

    for y in range(2):
        design_out[y] = wide_design[1 + y]
        node_out[y] = wide_node[1 + y]
    for copy in copies:
        copy.wait_send()


def backward_kernel(final, pulled, design, node, previous, sensitivity, grads, slopes, sem):
    copies = []
    for y in range(2):
        f = [final[i, y] for i in range(27)]
        kind = node[y]
        _, pull = jax.vjp(lambda pops, field, kind=kind: collide(pops, field, kind), f, design[y])
        values, slopes[y] = pull([pulled[i, y] for i in range(27)])
        for i in range(27):
            grads[y, i] = values[i]
        copies.append(pltpu.make_async_copy(grads.at[y], previous.at[:, y], sem.at[y]))
        copies[-1].start()
    copies.append(pltpu.make_async_copy(slopes, sensitivity, sem.at[2]))
    copies[-1].start()
    for copy in copies:
        copy.wait()


def solution(mesh):
    counts = (mesh.shape["gy"], mesh.shape["gz"])

    def local(ckpt_pops, adjoint_pops, design, node_types):
        f32 = jnp.float32
        cells = ckpt_pops.shape[1:]
        hbm = pl.BlockSpec(memory_space=pltpu.HBM)
        vmem = pl.BlockSpec(memory_space=pltpu.VMEM)
        slabs = (27,) + cells
        gathered = pl.pallas_call(
            lambda *refs: gather_kernel(counts, *refs),
            out_shape=(
                pltpu.VMEM(slabs, f32),
                pltpu.VMEM(slabs, f32),
                pltpu.VMEM(cells, f32),
                pltpu.VMEM(cells, jnp.int32),
            ),
            in_specs=[hbm] * 4,
            out_specs=[vmem] * 4,
            scratch_shapes=[
                pltpu.VMEM((3, 3, 3) + cells, f32),
                pltpu.VMEM((3, 3, 3) + cells, f32),
                pltpu.VMEM((6, 3, 3, 8, 128), f32),
                pltpu.VMEM((27, 5, 8, 128), f32),
                pltpu.VMEM((5, 8, 128), f32),
                pltpu.VMEM((5, 8, 128), jnp.int32),
                pltpu.VMEM((27, 5, 8, 128), f32),
                pltpu.VMEM((2, 3, 3, 3, 8, 128), f32),
                pltpu.VMEM((2, 3, 3, 8, 128), f32),
                pltpu.VMEM((2, 80, 128), f32),
                pltpu.VMEM((2, 80, 128), f32),
                pltpu.VMEM((4, 32, 128), f32),
                pltpu.SemaphoreType.DMA((4,)),
                pltpu.SemaphoreType.DMA((18,)),
                pltpu.SemaphoreType.DMA((18,)),
            ],
            compiler_params=pltpu.CompilerParams(
                collective_id=0, has_side_effects=True, vmem_limit_bytes=16 * 2**20
            ),
            name="gather_cells",
        )(
            *[
                pltpu.with_memory_space_constraint(array, pltpu.HBM)
                for array in (
                    ckpt_pops.reshape((3, 3, 3) + cells),
                    adjoint_pops.reshape((3, 3, 3) + cells),
                    design,
                    node_types,
                )
            ]
        )
        return pl.pallas_call(
            backward_kernel,
            out_shape=(
                jax.ShapeDtypeStruct(slabs, f32),
                jax.ShapeDtypeStruct(cells, f32),
            ),
            in_specs=[vmem] * 4,
            out_specs=[hbm] * 2,
            scratch_shapes=[
                pltpu.VMEM((2, 27, 8, 128), f32),
                pltpu.VMEM((2, 8, 128), f32),
                pltpu.SemaphoreType.DMA((3,)),
            ],
            compiler_params=pltpu.CompilerParams(vmem_limit_bytes=16 * 2**20),
            name="backward_cells",
        )(*gathered)

    return jax.shard_map(
        local,
        mesh=mesh,
        in_specs=(
            P(None, "gy", "gz", None),
            P(None, "gy", "gz", None),
            P("gy", "gz", None),
            P("gy", "gz", None),
        ),
        out_specs=(P(None, "gy", "gz", None), P("gy", "gz", None)),
        check_vma=False,
    )
```

```python
import jax
import jax.numpy as jnp
from jax import lax
from jax.experimental import pallas as pl
from jax.experimental.pallas import tpu as pltpu
from jax.sharding import PartitionSpec as P

relax_rate = 1.0 / 0.6
brinkman = 4.0
inflow = 0.05

MESH = pl.DeviceIdType.MESH
SIDES = [(1, 0), (-1, 0), (0, 1), (0, -1), (1, 1), (1, -1), (-1, 1), (-1, -1)]


def full(like, value):
    return jnp.full(like.shape, value, like.dtype)


def rebuild_line(zeroth, linear, square, shift):
    if zeroth is None:
        twice = shift * (linear + linear)
        if square is not None:
            twice = twice + square
        return 0.5 * (twice - linear), -twice, 0.5 * (twice + linear)
    odd = shift * zeroth
    if linear is None:
        even = shift * odd
    else:
        odd = odd + linear
        even = shift * (odd + linear)
    if square is not None:
        even = even + square
    return 0.5 * (even - odd), zeroth - even, 0.5 * (even + odd)


def collide(f, design, node):
    z0, z1, z2 = [], [], []
    for ab in range(9):
        lower, middle, upper = f[3 * ab : 3 * ab + 3]
        ends = upper + lower
        z0.append(ends + middle)
        z1.append(upper - lower)
        z2.append(ends)
    y00, y10, y20, y01, y11, y02 = [], [], [], [], [], []
    for a in range(3):
        ends = z0[3 * a + 2] + z0[3 * a]
        y00.append(ends + z0[3 * a + 1])
        y10.append(z0[3 * a + 2] - z0[3 * a])
        y20.append(ends)
        y01.append(z1[3 * a] + z1[3 * a + 1] + z1[3 * a + 2])
        y11.append(z1[3 * a + 2] - z1[3 * a])
        y02.append(z2[3 * a] + z2[3 * a + 1] + z2[3 * a + 2])
    m200 = y00[2] + y00[0]
    rho = m200 + y00[1]
    jx = y00[2] - y00[0]
    jy = y10[0] + y10[1] + y10[2]
    m110 = y10[2] - y10[0]
    m020 = y20[0] + y20[1] + y20[2]
    jz = y01[0] + y01[1] + y01[2]
    m101 = y01[2] - y01[0]
    m011 = y11[0] + y11[1] + y11[2]
    m002 = y02[0] + y02[1] + y02[2]

    inverse = 1.0 / rho
    ux, uy, uz = jx * inverse, jy * inverse, jz * inverse
    keep_rate = 1.0 - relax_rate
    base = (relax_rate / 3.0) * rho
    sxx = keep_rate * (m200 - jx * ux) + base
    syy = keep_rate * (m020 - jy * uy) + base
    szz = keep_rate * (m002 - jz * uz) + base
    sxy = keep_rate * (m110 - jx * uy)
    sxz = keep_rate * (m101 - jx * uz)
    syz = keep_rate * (m011 - jy * uz)

    fluid = node == 0
    one, nought, third = full(rho, 1.0), full(rho, 0.0), full(rho, 1.0 / 3.0)
    rho = lax.select(fluid, rho, one)
    inverse = lax.select(fluid, inverse, one)
    sxx = lax.select(fluid, sxx, third)
    syy = lax.select(fluid, syy, third)
    szz = lax.select(fluid, szz, third)
    sxy = lax.select(fluid, sxy, nought)
    sxz = lax.select(fluid, sxz, nought)
    syz = lax.select(fluid, syz, nought)
    keeping = 1.0 / (1.0 + brinkman * (1.0 - design))
    factor = lax.select(fluid, keeping, lax.select(node == 3, one, nought))
    vx = ux * factor + lax.select(node == 2, full(rho, inflow), nought)
    vy = uy * factor
    vz = uz * factor

    dxy, dxz, dyz = sxy + sxy, sxz + sxz, syz + syz
    fxy, fxz, fyz = dxy * sxy, dxz * sxz, dyz * syz
    g220 = (sxx * syy + fxy) * inverse
    g202 = (sxx * szz + fxz) * inverse
    g022 = (syy * szz + fyz) * inverse
    g211 = (sxx * syz + dxy * sxz) * inverse
    g121 = (syy * sxz + dxy * syz) * inverse
    g112 = (szz * sxy + dxz * syz) * inverse
    g222 = (
        (sxx * (syy * szz + fyz) + syy * fxz + szz * fxy + 2.0 * (dxy * dxz) * syz)
        * inverse
        * inverse
    )
    lines = {
        (0, 0): (rho, None, szz),
        (2, 0): (sxx, None, g202),
        (0, 2): (syy, None, g022),
        (2, 2): (g220, None, g222),
        (1, 1): (sxy, None, g112),
        (1, 0): (None, sxz, None),
        (0, 1): (None, syz, None),
        (2, 1): (None, g211, None),
        (1, 2): (None, g121, None),
    }
    along_z = {key: rebuild_line(*value, vz) for key, value in lines.items()}
    result = [None] * 27
    along_y = {
        (p, c): rebuild_line(along_z[p, 0][c], along_z[p, 1][c], along_z[p, 2][c], vy)
        for p in range(3)
        for c in range(3)
    }
    for b in range(3):
        for c in range(3):
            line = rebuild_line(along_y[0, c][b], along_y[1, c][b], along_y[2, c][b], vx)
            for a in range(3):
                result[9 * a + 3 * b + c] = line[a]
    solid = node == 1
    return [lax.select(solid, f[26 - i], result[i]) for i in range(27)]


def edge(step, last):
    return last if step > 0 else 0


GROUPS = {1: [(1, 1), (2, 0), (2, 1)], -1: [(0, 0), (0, 1), (1, 0)]}
CELL_ROW, BACK_ROW = 54, 58
KEPT = [(1, 0), (1, 1), (2, 0), (0, 1)]
TURNS = (1, -1)


def moving(step, kind):
    near, far = (7, 6) if step > 0 else (0, 1)
    return [(far, 1 + step), (near, 1), (near, 1 + step)][kind]


def pack(tile, back, design, node, rows_z, rows_d):
    for way, step in enumerate(TURNS):
        near = edge(step, 7)
        for kind in range(3):
            z, c = moving(step, kind)
            for y in range(2):
                for b in range(3):
                    for a in range(3):
                        k = 18 * kind + 9 * y + 3 * b + a
                        rows_z[way, k : k + 1, :] = tile(a, b, c, y)[z : z + 1, :]
        for y in range(2):
            k = CELL_ROW + 2 * y
            rows_z[way, k : k + 1, :] = design[1 + y, near : near + 1, :]
            rows_z[way, k + 1 : k + 2, :] = node[1 + y, near : near + 1, :].astype(jnp.float32)
        for k, (b, y) in enumerate(KEPT):
            for a in range(3):
                at = BACK_ROW + 3 * k + a
                rows_z[way, at : at + 1, :] = back(a, b, 1 + step, y)[near : near + 1, :]
        for turn, step_y in enumerate(TURNS):
            corner = 2 * turn + way
            for kind in range(3):
                z, c = moving(step, kind)
                for j, (b, y) in enumerate(GROUPS[step_y]):
                    for a in range(3):
                        k = 9 * kind + 3 * j + a
                        rows_d[corner, k : k + 1, :] = tile(a, b, c, y)[z : z + 1, :]
            y = edge(step_y, 1)
            rows_d[corner, 27:28, :] = design[1 + y, near : near + 1, :]
            rows_d[corner, 28:29, :] = node[1 + y, near : near + 1, :].astype(jnp.float32)
            for a in range(3):
                rows_d[corner, 29 + a : 30 + a, :] = back(a, 1 + step_y, 1 + step, y)[
                    near : near + 1, :
                ]


def shifted(value, a, c, line, row):
    if c != 1:
        value = pltpu.roll(value, 1 if c == 2 else 7, 0)
        value = jnp.where(row == (0 if c == 2 else 7), line, value)
    if a != 1:
        value = pltpu.roll(value, 1 if a == 2 else 127, 1)
    return value


def gather_kernel(
    counts,
    ckpt_in,
    adjoint_in,
    design_in,
    node_in,
    final,
    pulled,
    design_out,
    node_out,
    ckpt,
    adjoint,
    post,
    primal,
    wide_design,
    wide_node,
    second,
    got_y,
    got_back,
    put_z,
    got_z,
    put_d,
    got_d,
    load_sem,
    send_sem,
    recv_sem,
):
    gy, gz = lax.axis_index("gy"), lax.axis_index("gz")
    near = [
        (lax.rem(gy + dy + counts[0], counts[0]), lax.rem(gz + dz + counts[1], counts[1]))
        for dy, dz in SIDES
    ]
    barrier = pltpu.get_barrier_semaphore()
    for who in near:
        pl.semaphore_signal(barrier, inc=1, device_id=who, device_id_type=MESH)

    loads = [
        pltpu.make_async_copy(src, dst, load_sem.at[i])
        for i, (src, dst) in enumerate(
            [
                (ckpt_in, ckpt),
                (design_in, wide_design.at[pl.ds(1, 2)]),
                (node_in, wide_node.at[pl.ds(1, 2)]),
                (adjoint_in, adjoint),
            ]
        )
    ]
    for load in loads:
        load.start()
    row = lax.broadcasted_iota(jnp.int32, (8, 128), 0)
    for load in loads[:3]:
        load.wait()

    def collide_first(y, carry):
        f = [ckpt[i // 9, i // 3 % 3, i % 3, y] for i in range(27)]
        h = collide(f, wide_design[1 + y], wide_node[1 + y])
        for i in range(27):
            post[2 * (i // 3 % 3) + y, i // 9, i % 3] = h[i]
        return carry

    lax.fori_loop(0, 2, collide_first, 0)

    def own(a, b, c, y):
        return post[2 * b + y, a, c]

    def back(a, b, c, y):
        return adjoint[2 - a, 2 - b, 2 - c, y]

    loads[3].wait()
    pack(own, back, wide_design, wide_node, put_z, put_d)

    plan = [(put_d.at[i], got_d.at[i], 4 + i) for i in range(4)]
    plan += [(post.at[pl.ds(3 - 3 * turn, 3)], got_y.at[turn], turn) for turn in range(2)]
    for turn, y in enumerate((1, 0)):
        plan += [
            (wide_design.at[1 + y], wide_design.at[3 * turn], turn),
            (wide_node.at[1 + y], wide_node.at[3 * turn], turn),
        ]
    plan += [(put_z.at[i], got_z.at[i], 2 + i) for i in range(2)]
    plan += [(adjoint.at[:, 2 * turn, :, 1 - turn], got_back.at[turn], turn) for turn in range(2)]
    copies = [
        pltpu.make_async_remote_copy(
            src_ref=src,
            dst_ref=dst,
            send_sem=send_sem.at[i],
            recv_sem=recv_sem.at[i],
            device_id=near[who],
            device_id_type=MESH,
        )
        for i, (src, dst, who) in enumerate(plan)
    ]
    pl.semaphore_wait(barrier, len(near))
    for copy in copies:
        copy.start()
    for copy in copies[:12]:
        copy.wait_recv()

    def outer(a, b, c, y):
        if 0 <= y < 2:
            return own(a, b, c, y)
        turn = 0 if y < 0 else 1
        return got_y[turn, GROUPS[TURNS[turn]].index((b, y + 2 if y < 0 else y - 2)), a, c]

    def edge_row(kind, a, b, y, way):
        if 0 <= y < 2:
            k = 18 * kind + 9 * y + 3 * b + a
            return got_z[way, k : k + 1, :]
        turn = 0 if y < 0 else 1
        j = GROUPS[TURNS[turn]].index((b, y + 2 if y < 0 else y - 2))
        k = 9 * kind + 3 * j + a
        return got_d[2 * turn + way, k : k + 1, :]

    def stack_rows(lines):
        value = jnp.broadcast_to(lines[0], (8, 128))
        for r in range(1, 8):
            value = jnp.where(row == r, lines[r], value)
        return value

    for i in range(27):
        a, b, c = i // 9, i // 3 % 3, i % 3
        for t in range(4):
            y = t - b
            line = None if c == 1 else edge_row(2, a, b, y, 0 if c == 2 else 1)
            primal[i, t] = shifted(outer(a, b, c, y), a, c, line, row)
        lines = []
        for way in range(2):
            for t in range(4):
                y = t - b
                if c == 1:
                    lines.append(edge_row(1, a, b, y, way))
                elif (c == 2) == (way == 0):
                    lines.append(edge_row(0, a, b, y, way))
                else:
                    z = 0 if way == 0 else 7
                    lines.append(outer(a, b, c, y)[z : z + 1, :])
        primal[i, 4] = shifted(stack_rows(lines), a, 1, None, row)
    columns = []
    for part in range(2):
        lines = []
        for way in range(2):
            lines.append(got_d[way, 27 + part : 28 + part, :])
            for y in range(2):
                k = CELL_ROW + 2 * y + part
                lines.append(got_z[way, k : k + 1, :])
            lines.append(got_d[2 + way, 27 + part : 28 + part, :])
        columns.append(stack_rows(lines))
    wide_design[4] = columns[0]
    one, nought = jnp.ones_like(row), jnp.zeros_like(row)
    kind = jnp.where(columns[1] == 3.0, one + one + one, nought)
    kind = jnp.where(columns[1] == 2.0, one + one, kind)
    wide_node[4] = jnp.where(columns[1] == 1.0, one, kind)

    def collide_second(t, carry):
        f = [primal[i, t] for i in range(27)]
        h = collide(f, wide_design[t], wide_node[t])
        for i in range(27):
            second[i, t] = h[i]
        return carry

    lax.fori_loop(0, 5, collide_second, 0)

    for copy in copies[12:]:
        copy.wait_recv()
    for i in range(27):
        a, b, c = i // 9, i // 3 % 3, i % 3
        way = 0 if c == 2 else 1
        for y in range(2):
            t = y - b + 2
            r = t + 4 * way
            line = None if c == 1 else second[i, 4, r : r + 1, :]
            final[i, y] = shifted(second[i, t], a, c, line, row)

            source = y - (b - 1)
            if 0 <= source < 2:
                value = back(a, b, c, source)
                k = BACK_ROW + 3 * KEPT.index((b, source)) + a if c != 1 else 0
                line = got_z[way, k : k + 1, :]
            else:
                turn = 0 if b == 2 else 1
                value = got_back[turn, 2 - a, 2 - c]
                line = got_d[2 * turn + way, 29 + a : 30 + a, :]
            pulled[26 - i, y] = shifted(value, a, c, line, row)

    for y in range(2):
        design_out[y] = wide_design[1 + y]
        node_out[y] = wide_node[1 + y]
    for copy in copies:
        copy.wait_send()


def backward_kernel(final, pulled, design, node, previous, sensitivity, grads, slopes, sem):
    copies = []
    for y in range(2):
        f = [final[i, y] for i in range(27)]
        kind = node[y]
        _, pull = jax.vjp(lambda pops, field, kind=kind: collide(pops, field, kind), f, design[y])
        values, slopes[y] = pull([pulled[i, y] for i in range(27)])
        for i in range(27):
            grads[y, i] = values[i]
        copies.append(pltpu.make_async_copy(grads.at[y], previous.at[:, y], sem.at[y]))
        copies[-1].start()
    copies.append(pltpu.make_async_copy(slopes, sensitivity, sem.at[2]))
    copies[-1].start()
    for copy in copies:
        copy.wait()


def solution(mesh):
    counts = (mesh.shape["gy"], mesh.shape["gz"])

    def local(ckpt_pops, adjoint_pops, design, node_types):
        f32 = jnp.float32
        cells = ckpt_pops.shape[1:]
        hbm = pl.BlockSpec(memory_space=pltpu.HBM)
        vmem = pl.BlockSpec(memory_space=pltpu.VMEM)
        slabs = (27,) + cells
        gathered = pl.pallas_call(
            lambda *refs: gather_kernel(counts, *refs),
            out_shape=(
                pltpu.VMEM(slabs, f32),
                pltpu.VMEM(slabs, f32),
                pltpu.VMEM(cells, f32),
                pltpu.VMEM(cells, jnp.int32),
            ),
            in_specs=[hbm] * 4,
            out_specs=[vmem] * 4,
            scratch_shapes=[
                pltpu.VMEM((3, 3, 3) + cells, f32),
                pltpu.VMEM((3, 3, 3) + cells, f32),
                pltpu.VMEM((6, 3, 3, 8, 128), f32),
                pltpu.VMEM((27, 5, 8, 128), f32),
                pltpu.VMEM((5, 8, 128), f32),
                pltpu.VMEM((5, 8, 128), jnp.int32),
                pltpu.VMEM((27, 5, 8, 128), f32),
                pltpu.VMEM((2, 3, 3, 3, 8, 128), f32),
                pltpu.VMEM((2, 3, 3, 8, 128), f32),
                pltpu.VMEM((2, 72, 128), f32),
                pltpu.VMEM((2, 72, 128), f32),
                pltpu.VMEM((4, 32, 128), f32),
                pltpu.VMEM((4, 32, 128), f32),
                pltpu.SemaphoreType.DMA((4,)),
                pltpu.SemaphoreType.DMA((14,)),
                pltpu.SemaphoreType.DMA((14,)),
            ],
            compiler_params=pltpu.CompilerParams(
                collective_id=0, has_side_effects=True, vmem_limit_bytes=16 * 2**20
            ),
            name="gather_cells",
        )(
            *[
                pltpu.with_memory_space_constraint(array, pltpu.HBM)
                for array in (
                    ckpt_pops.reshape((3, 3, 3) + cells),
                    adjoint_pops.reshape((3, 3, 3) + cells),
                    design,
                    node_types,
                )
            ]
        )
        return pl.pallas_call(
            backward_kernel,
            out_shape=(
                jax.ShapeDtypeStruct(slabs, f32),
                jax.ShapeDtypeStruct(cells, f32),
            ),
            in_specs=[vmem] * 4,
            out_specs=[hbm] * 2,
            scratch_shapes=[
                pltpu.VMEM((2, 27, 8, 128), f32),
                pltpu.VMEM((2, 8, 128), f32),
                pltpu.SemaphoreType.DMA((3,)),
            ],
            compiler_params=pltpu.CompilerParams(vmem_limit_bytes=16 * 2**20),
            name="backward_cells",
        )(*gathered)

    return jax.shard_map(
        local,
        mesh=mesh,
        in_specs=(
            P(None, "gy", "gz", None),
            P(None, "gy", "gz", None),
            P("gy", "gz", None),
            P("gy", "gz", None),
        ),
        out_specs=(P(None, "gy", "gz", None), P("gy", "gz", None)),
        check_vma=False,
    )
```

```python
import jax
import jax.numpy as jnp
from jax import lax
from jax.experimental import pallas as pl
from jax.experimental.pallas import tpu as pltpu
from jax.sharding import PartitionSpec as P

relax_rate = 1.0 / 0.6
brinkman = 4.0
inflow = 0.05

MESH = pl.DeviceIdType.MESH
SIDES = [(1, 0), (-1, 0), (0, 1), (0, -1), (1, 1), (1, -1), (-1, 1), (-1, -1)]


def full(like, value):
    return jnp.full(like.shape, value, like.dtype)


def rebuild_line(zeroth, linear, square, shift):
    if zeroth is None:
        twice = shift * (linear + linear)
        if square is not None:
            twice = twice + square
        return 0.5 * (twice - linear), -twice, 0.5 * (twice + linear)
    odd = shift * zeroth
    if linear is None:
        even = shift * odd
    else:
        odd = odd + linear
        even = shift * (odd + linear)
    if square is not None:
        even = even + square
    return 0.5 * (even - odd), zeroth - even, 0.5 * (even + odd)


def collide(f, design, node):
    z0, z1, z2 = [], [], []
    for ab in range(9):
        lower, middle, upper = f[3 * ab : 3 * ab + 3]
        ends = upper + lower
        z0.append(ends + middle)
        z1.append(upper - lower)
        z2.append(ends)
    y00, y10, y20, y01, y11, y02 = [], [], [], [], [], []
    for a in range(3):
        ends = z0[3 * a + 2] + z0[3 * a]
        y00.append(ends + z0[3 * a + 1])
        y10.append(z0[3 * a + 2] - z0[3 * a])
        y20.append(ends)
        y01.append(z1[3 * a] + z1[3 * a + 1] + z1[3 * a + 2])
        y11.append(z1[3 * a + 2] - z1[3 * a])
        y02.append(z2[3 * a] + z2[3 * a + 1] + z2[3 * a + 2])
    m200 = y00[2] + y00[0]
    rho = m200 + y00[1]
    jx = y00[2] - y00[0]
    jy = y10[0] + y10[1] + y10[2]
    m110 = y10[2] - y10[0]
    m020 = y20[0] + y20[1] + y20[2]
    jz = y01[0] + y01[1] + y01[2]
    m101 = y01[2] - y01[0]
    m011 = y11[0] + y11[1] + y11[2]
    m002 = y02[0] + y02[1] + y02[2]

    inverse = 1.0 / rho
    ux, uy, uz = jx * inverse, jy * inverse, jz * inverse
    keep_rate = 1.0 - relax_rate
    base = (relax_rate / 3.0) * rho
    sxx = keep_rate * (m200 - jx * ux) + base
    syy = keep_rate * (m020 - jy * uy) + base
    szz = keep_rate * (m002 - jz * uz) + base
    sxy = keep_rate * (m110 - jx * uy)
    sxz = keep_rate * (m101 - jx * uz)
    syz = keep_rate * (m011 - jy * uz)

    fluid = node == 0
    one, nought, third = full(rho, 1.0), full(rho, 0.0), full(rho, 1.0 / 3.0)
    rho = lax.select(fluid, rho, one)
    inverse = lax.select(fluid, inverse, one)
    sxx = lax.select(fluid, sxx, third)
    syy = lax.select(fluid, syy, third)
    szz = lax.select(fluid, szz, third)
    sxy = lax.select(fluid, sxy, nought)
    sxz = lax.select(fluid, sxz, nought)
    syz = lax.select(fluid, syz, nought)
    keeping = 1.0 / (1.0 + brinkman * (1.0 - design))
    factor = lax.select(fluid, keeping, lax.select(node == 3, one, nought))
    vx = ux * factor + lax.select(node == 2, full(rho, inflow), nought)
    vy = uy * factor
    vz = uz * factor

    dxy, dxz, dyz = sxy + sxy, sxz + sxz, syz + syz
    fxy, fxz, fyz = dxy * sxy, dxz * sxz, dyz * syz
    g220 = (sxx * syy + fxy) * inverse
    g202 = (sxx * szz + fxz) * inverse
    g022 = (syy * szz + fyz) * inverse
    g211 = (sxx * syz + dxy * sxz) * inverse
    g121 = (syy * sxz + dxy * syz) * inverse
    g112 = (szz * sxy + dxz * syz) * inverse
    g222 = (
        (sxx * (syy * szz + fyz) + syy * fxz + szz * fxy + 2.0 * (dxy * dxz) * syz)
        * inverse
        * inverse
    )
    lines = {
        (0, 0): (rho, None, szz),
        (2, 0): (sxx, None, g202),
        (0, 2): (syy, None, g022),
        (2, 2): (g220, None, g222),
        (1, 1): (sxy, None, g112),
        (1, 0): (None, sxz, None),
        (0, 1): (None, syz, None),
        (2, 1): (None, g211, None),
        (1, 2): (None, g121, None),
    }
    along_z = {key: rebuild_line(*value, vz) for key, value in lines.items()}
    result = [None] * 27
    along_y = {
        (p, c): rebuild_line(along_z[p, 0][c], along_z[p, 1][c], along_z[p, 2][c], vy)
        for p in range(3)
        for c in range(3)
    }
    for b in range(3):
        for c in range(3):
            line = rebuild_line(along_y[0, c][b], along_y[1, c][b], along_y[2, c][b], vx)
            for a in range(3):
                result[9 * a + 3 * b + c] = line[a]
    solid = node == 1
    return [lax.select(solid, f[26 - i], result[i]) for i in range(27)]


def edge(step, last):
    return last if step > 0 else 0


GROUPS = {1: [(1, 1), (2, 0), (2, 1)], -1: [(0, 0), (0, 1), (1, 0)]}
CELL_ROW, BACK_ROW = 54, 58
KEPT = [(1, 0), (1, 1), (2, 0), (0, 1)]
TURNS = (1, -1)


def moving(step, kind):
    near, far = (7, 6) if step > 0 else (0, 1)
    return [(far, 1 + step), (near, 1), (near, 1 + step)][kind]


def pack(tile, back, design, node, rows_z, rows_d):
    for way, step in enumerate(TURNS):
        near = edge(step, 7)
        for kind in range(3):
            z, c = moving(step, kind)
            for y in range(2):
                for b in range(3):
                    for a in range(3):
                        k = 18 * kind + 9 * y + 3 * b + a
                        rows_z[way, k : k + 1, :] = tile(a, b, c, y)[z : z + 1, :]
        for y in range(2):
            k = CELL_ROW + 2 * y
            rows_z[way, k : k + 1, :] = design[1 + y, near : near + 1, :]
            rows_z[way, k + 1 : k + 2, :] = node[1 + y, near : near + 1, :].astype(jnp.float32)
        for k, (b, y) in enumerate(KEPT):
            for a in range(3):
                at = BACK_ROW + 3 * k + a
                rows_z[way, at : at + 1, :] = back(a, b, 1 + step, y)[near : near + 1, :]
        for turn, step_y in enumerate(TURNS):
            corner = 2 * turn + way
            for kind in range(3):
                z, c = moving(step, kind)
                for j, (b, y) in enumerate(GROUPS[step_y]):
                    for a in range(3):
                        k = 9 * kind + 3 * j + a
                        rows_d[corner, k : k + 1, :] = tile(a, b, c, y)[z : z + 1, :]
            y = edge(step_y, 1)
            rows_d[corner, 27:28, :] = design[1 + y, near : near + 1, :]
            rows_d[corner, 28:29, :] = node[1 + y, near : near + 1, :].astype(jnp.float32)
            for a in range(3):
                rows_d[corner, 29 + a : 30 + a, :] = back(a, 1 + step_y, 1 + step, y)[
                    near : near + 1, :
                ]


def shifted(value, a, c, line, row):
    if c != 1:
        value = pltpu.roll(value, 1 if c == 2 else 7, 0)
        value = jnp.where(row == (0 if c == 2 else 7), line, value)
    if a != 1:
        value = pltpu.roll(value, 1 if a == 2 else 127, 1)
    return value


def gather_kernel(
    counts,
    ckpt_in,
    adjoint_in,
    design_in,
    node_in,
    final,
    pulled,
    design_out,
    node_out,
    ckpt,
    adjoint,
    post,
    primal,
    wide_design,
    wide_node,
    second,
    got_y,
    got_back,
    put_z,
    got_z,
    put_d,
    got_d,
    load_sem,
    send_sem,
    recv_sem,
):
    gy, gz = lax.axis_index("gy"), lax.axis_index("gz")
    near = [
        (lax.rem(gy + dy + counts[0], counts[0]), lax.rem(gz + dz + counts[1], counts[1]))
        for dy, dz in SIDES
    ]
    barrier = pltpu.get_barrier_semaphore()
    for who in reversed(near):
        pl.semaphore_signal(barrier, inc=1, device_id=who, device_id_type=MESH)

    loads = [
        pltpu.make_async_copy(src, dst, load_sem.at[i])
        for i, (src, dst) in enumerate(
            [
                (ckpt_in, ckpt),
                (design_in, wide_design.at[pl.ds(1, 2)]),
                (node_in, wide_node.at[pl.ds(1, 2)]),
                (adjoint_in, adjoint),
            ]
        )
    ]
    for load in loads:
        load.start()
    row = lax.broadcasted_iota(jnp.int32, (8, 128), 0)
    for load in loads[:3]:
        load.wait()

    def collide_first(y, carry):
        f = [ckpt[i // 9, i // 3 % 3, i % 3, y] for i in range(27)]
        h = collide(f, wide_design[1 + y], wide_node[1 + y])
        for i in range(27):
            post[2 * (i // 3 % 3) + y, i // 9, i % 3] = h[i]
        return carry

    lax.fori_loop(0, 2, collide_first, 0)

    def own(a, b, c, y):
        return post[2 * b + y, a, c]

    def back(a, b, c, y):
        return adjoint[2 - a, 2 - b, 2 - c, y]

    loads[3].wait()
    pack(own, back, wide_design, wide_node, put_z, put_d)

    plan = [(put_d.at[i], got_d.at[i], 4 + i) for i in range(4)]
    plan += [(post.at[pl.ds(3 - 3 * turn, 3)], got_y.at[turn], turn) for turn in range(2)]
    for turn, y in enumerate((1, 0)):
        plan += [
            (wide_design.at[1 + y], wide_design.at[3 * turn], turn),
            (wide_node.at[1 + y], wide_node.at[3 * turn], turn),
        ]
    plan += [(put_z.at[i], got_z.at[i], 2 + i) for i in range(2)]
    plan += [(adjoint.at[:, 2 * turn, :, 1 - turn], got_back.at[turn], turn) for turn in range(2)]
    copies = [
        pltpu.make_async_remote_copy(
            src_ref=src,
            dst_ref=dst,
            send_sem=send_sem.at[i],
            recv_sem=recv_sem.at[i],
            device_id=near[who],
            device_id_type=MESH,
        )
        for i, (src, dst, who) in enumerate(plan)
    ]
    pl.semaphore_wait(barrier, len(near))
    for copy in copies:
        copy.start()
    for copy in copies[:12]:
        copy.wait_recv()

    def outer(a, b, c, y):
        if 0 <= y < 2:
            return own(a, b, c, y)
        turn = 0 if y < 0 else 1
        return got_y[turn, GROUPS[TURNS[turn]].index((b, y + 2 if y < 0 else y - 2)), a, c]

    def edge_row(kind, a, b, y, way):
        if 0 <= y < 2:
            k = 18 * kind + 9 * y + 3 * b + a
            return got_z[way, k : k + 1, :]
        turn = 0 if y < 0 else 1
        j = GROUPS[TURNS[turn]].index((b, y + 2 if y < 0 else y - 2))
        k = 9 * kind + 3 * j + a
        return got_d[2 * turn + way, k : k + 1, :]

    def stack_rows(lines):
        value = jnp.broadcast_to(lines[0], (8, 128))
        for r in range(1, 8):
            value = jnp.where(row == r, lines[r], value)
        return value

    for i in range(27):
        a, b, c = i // 9, i // 3 % 3, i % 3
        for t in range(4):
            y = t - b
            line = None if c == 1 else edge_row(2, a, b, y, 0 if c == 2 else 1)
            primal[i, t] = shifted(outer(a, b, c, y), a, c, line, row)
        lines = []
        for way in range(2):
            for t in range(4):
                y = t - b
                if c == 1:
                    lines.append(edge_row(1, a, b, y, way))
                elif (c == 2) == (way == 0):
                    lines.append(edge_row(0, a, b, y, way))
                else:
                    z = 0 if way == 0 else 7
                    lines.append(outer(a, b, c, y)[z : z + 1, :])
        primal[i, 4] = shifted(stack_rows(lines), a, 1, None, row)
    columns = []
    for part in range(2):
        lines = []
        for way in range(2):
            lines.append(got_d[way, 27 + part : 28 + part, :])
            for y in range(2):
                k = CELL_ROW + 2 * y + part
                lines.append(got_z[way, k : k + 1, :])
            lines.append(got_d[2 + way, 27 + part : 28 + part, :])
        columns.append(stack_rows(lines))
    wide_design[4] = columns[0]
    one, nought = jnp.ones_like(row), jnp.zeros_like(row)
    kind = jnp.where(columns[1] == 3.0, one + one + one, nought)
    kind = jnp.where(columns[1] == 2.0, one + one, kind)
    wide_node[4] = jnp.where(columns[1] == 1.0, one, kind)

    def collide_second(t, carry):
        f = [primal[i, t] for i in range(27)]
        h = collide(f, wide_design[t], wide_node[t])
        for i in range(27):
            second[i, t] = h[i]
        return carry

    lax.fori_loop(0, 5, collide_second, 0)

    for copy in copies[12:]:
        copy.wait_recv()
    for i in range(27):
        a, b, c = i // 9, i // 3 % 3, i % 3
        way = 0 if c == 2 else 1
        for y in range(2):
            t = y - b + 2
            r = t + 4 * way
            line = None if c == 1 else second[i, 4, r : r + 1, :]
            final[i, y] = shifted(second[i, t], a, c, line, row)

            source = y - (b - 1)
            if 0 <= source < 2:
                value = back(a, b, c, source)
                k = BACK_ROW + 3 * KEPT.index((b, source)) + a if c != 1 else 0
                line = got_z[way, k : k + 1, :]
            else:
                turn = 0 if b == 2 else 1
                value = got_back[turn, 2 - a, 2 - c]
                line = got_d[2 * turn + way, 29 + a : 30 + a, :]
            pulled[26 - i, y] = shifted(value, a, c, line, row)

    for y in range(2):
        design_out[y] = wide_design[1 + y]
        node_out[y] = wide_node[1 + y]
    for copy in copies:
        copy.wait_send()


def backward_kernel(final, pulled, design, node, previous, sensitivity, grads, slopes, sem):
    copies = []
    for y in range(2):
        f = [final[i, y] for i in range(27)]
        kind = node[y]
        _, pull = jax.vjp(lambda pops, field, kind=kind: collide(pops, field, kind), f, design[y])
        values, slopes[y] = pull([pulled[i, y] for i in range(27)])
        for i in range(27):
            grads[y, i] = values[i]
        copies.append(pltpu.make_async_copy(grads.at[y], previous.at[:, y], sem.at[y]))
        copies[-1].start()
    copies.append(pltpu.make_async_copy(slopes, sensitivity, sem.at[2]))
    copies[-1].start()
    for copy in copies:
        copy.wait()


def solution(mesh):
    counts = (mesh.shape["gy"], mesh.shape["gz"])

    def local(ckpt_pops, adjoint_pops, design, node_types):
        f32 = jnp.float32
        cells = ckpt_pops.shape[1:]
        hbm = pl.BlockSpec(memory_space=pltpu.HBM)
        vmem = pl.BlockSpec(memory_space=pltpu.VMEM)
        slabs = (27,) + cells
        gathered = pl.pallas_call(
            lambda *refs: gather_kernel(counts, *refs),
            out_shape=(
                pltpu.VMEM(slabs, f32),
                pltpu.VMEM(slabs, f32),
                pltpu.VMEM(cells, f32),
                pltpu.VMEM(cells, jnp.int32),
            ),
            in_specs=[hbm] * 4,
            out_specs=[vmem] * 4,
            scratch_shapes=[
                pltpu.VMEM((3, 3, 3) + cells, f32),
                pltpu.VMEM((3, 3, 3) + cells, f32),
                pltpu.VMEM((6, 3, 3, 8, 128), f32),
                pltpu.VMEM((27, 5, 8, 128), f32),
                pltpu.VMEM((5, 8, 128), f32),
                pltpu.VMEM((5, 8, 128), jnp.int32),
                pltpu.VMEM((27, 5, 8, 128), f32),
                pltpu.VMEM((2, 3, 3, 3, 8, 128), f32),
                pltpu.VMEM((2, 3, 3, 8, 128), f32),
                pltpu.VMEM((2, 72, 128), f32),
                pltpu.VMEM((2, 72, 128), f32),
                pltpu.VMEM((4, 32, 128), f32),
                pltpu.VMEM((4, 32, 128), f32),
                pltpu.SemaphoreType.DMA((4,)),
                pltpu.SemaphoreType.DMA((14,)),
                pltpu.SemaphoreType.DMA((14,)),
            ],
            compiler_params=pltpu.CompilerParams(
                collective_id=0, has_side_effects=True, vmem_limit_bytes=16 * 2**20
            ),
            name="gather_cells",
        )(
            *[
                pltpu.with_memory_space_constraint(array, pltpu.HBM)
                for array in (
                    ckpt_pops.reshape((3, 3, 3) + cells),
                    adjoint_pops.reshape((3, 3, 3) + cells),
                    design,
                    node_types,
                )
            ]
        )
        return pl.pallas_call(
            backward_kernel,
            out_shape=(
                jax.ShapeDtypeStruct(slabs, f32),
                jax.ShapeDtypeStruct(cells, f32),
            ),
            in_specs=[vmem] * 4,
            out_specs=[hbm] * 2,
            scratch_shapes=[
                pltpu.VMEM((2, 27, 8, 128), f32),
                pltpu.VMEM((2, 8, 128), f32),
                pltpu.SemaphoreType.DMA((3,)),
            ],
            compiler_params=pltpu.CompilerParams(vmem_limit_bytes=16 * 2**20),
            name="backward_cells",
        )(*gathered)

    return jax.shard_map(
        local,
        mesh=mesh,
        in_specs=(
            P(None, "gy", "gz", None),
            P(None, "gy", "gz", None),
            P("gy", "gz", None),
            P("gy", "gz", None),
        ),
        out_specs=(P(None, "gy", "gz", None), P("gy", "gz", None)),
        check_vma=False,
    )
```
